256 devices in a mesh: view: 8 (over x, core), slab: 32 (over y, z).
Axes of the slice: x: 4, y: 4, z: 8, core: 2. Of those that a mesh axis runs over, the one named last changes fastest.
Arguments:
- image: float32 [128, 512, 512], P('slab'), may hold values from 0.1 to 10
- sensitivity: float32 [128, 512, 512], P('slab', 'view'), may hold values from 0.5 to 4
- resample_x: bfloat16 [16, 512, 512], P('view'), may hold values from 0 to 1, as said below
- resample_y: bfloat16 [16, 512, 512], P('view'), may hold values from 0 to 1, as said below
- tof_kernel: bfloat16 [16, 16, 512], P('view'), may hold values from 0.00019454956 to 0.0078125
- axial_mix: float32 [16, 128, 128], P('view'), may hold values from 0 to 1
- background: float32 [16, 16, 512, 128], P('view', None, 'slab'), may hold values from 0.5 to 2
- counts: int32 [16, 16, 512, 128], P('view', None, 'slab'), may hold values from 0 to 19
Outputs:
- new_image: float32 [128, 512, 512], P('slab', 'view')
The draws below stay inside these ranges and needn't reach their ends.
Inputs may be any that keep to these rules, and one draw needn't show every extreme that they name: resample_x[v, a, x] is zero where |x - a| > 3. resample_y[v, y, b] is zero where |b - y| > 3.
All inputs are finite; a program needn't handle non-finite values.
Results may differ from the reference program's by a relative error of at most 0.00052.
Values may be sent and summed in bfloat16 or wider, within the bound.
A program may use at most 64 MiB of HBM per device.

```python
import math
import jax
import jax.numpy as jnp
from jax import lax

NX = 512
NY = 512
TOF_BINS = 16
BAND = 3
VIEWS = 16
SLICES = 128


def banded_blur(key, cells):
    key_shift, key_width, key_factor = jax.random.split(key, 3)
    shift = jax.random.uniform(key_shift, (VIEWS, 1, 1), jnp.float32, -0.5, 0.5)
    width = jax.random.uniform(key_width, (VIEWS, 1, 1), jnp.float32, 0.7, 1.3)
    factor = jax.random.uniform(key_factor, (VIEWS, cells, cells), jnp.float32, 0.5, 1.5)
    row_index = jnp.arange(cells, dtype=jnp.int32)[:, None]
    col_index = jnp.arange(cells, dtype=jnp.int32)[None, :]
    offset = col_index - row_index
    inside = jnp.abs(offset) <= BAND
    distance = offset.astype(jnp.float32)[None]
    profile = jnp.exp(-(distance - shift) ** 2 / (2.0 * width * width))
    values = jnp.where(inside[None], 0.4 * factor * profile, 0.0)
    return values.astype(jnp.bfloat16)


def draw_resample_x(key, part):
    return banded_blur(jax.random.fold_in(key, 11), NX)


def draw_resample_y(key, part):
    return banded_blur(jax.random.fold_in(key, 23), NY)


def draw_axial_mix(key, part):
    key_spread, key_factor = jax.random.split(jax.random.fold_in(key, 37), 2)
    spread = jnp.exp(jax.random.uniform(key_spread, (VIEWS, 1, 1), jnp.float32, 0.0, 1.0) * jnp.log(SLICES / 8.0))
    factor = jax.random.uniform(key_factor, (VIEWS, SLICES, SLICES), jnp.float32, 0.5, 1.5)
    plane_index = jnp.arange(SLICES, dtype=jnp.int32)[:, None]
    slice_index = jnp.arange(SLICES, dtype=jnp.int32)[None, :]
    distance = (plane_index - slice_index).astype(jnp.float32)[None]
    profile = jnp.exp(-(distance * distance) / (2.0 * spread * spread))
    return 0.4 / spread * factor * profile


def set_ends(values, rng, smallest, largest):
    longest = values.shape.index(max(values.shape))
    spots = []
    for shift in (0, 1):
        where = [jax.random.randint(jax.random.fold_in(rng, axis), (), 0, length) for axis, length in enumerate(values.shape)]
        where[longest] = (where[longest] + shift) % values.shape[longest]
        spots.append(tuple(where))
    return values.at[spots[0]].set(smallest).at[spots[1]].set(largest)


def block_levels(key, extent, cuts, least, top_value):
    level, own = 1.0, jax.random.fold_in(key, 6)
    for axis_at, blocks in cuts:
        heights = jnp.exp(jax.random.uniform(jax.random.fold_in(own, axis_at), (blocks,), jnp.float32, least / len(cuts), top_value / len(cuts)))
        level = level * jnp.repeat(heights, extent[axis_at] // blocks).reshape([-1 if axis == axis_at else 1 for axis in range(len(extent))])
    return level


def setup_inputs(seed: int = 0) -> dict:
    arg_keys = jax.random.split(jax.random.key(seed), 9)
    image = jnp.clip(jnp.exp(math.log(10.0) - 4.6051702 * jax.random.uniform(arg_keys[0], (SLICES, NX, NY), jnp.float32) ** block_levels(arg_keys[0], (SLICES, NX, NY), ((0, 32),), -0.2, 0.2)), 0.1, 10.0)
    sensitivity = jnp.clip(jnp.exp(math.log(4.0) - 2.0794415 * jax.random.uniform(arg_keys[1], (SLICES, NX, NY), jnp.float32) ** block_levels(arg_keys[1], (SLICES, NX, NY), ((0, 32), (1, 8)), -0.2, 0.2)), 0.5, 4.0)
    resample_x = draw_resample_x(jax.random.fold_in(arg_keys[8], 71), 0)
    resample_y = draw_resample_y(jax.random.fold_in(arg_keys[8], 71), 0)
    tof_kernel = jnp.clip(jnp.exp(math.log(0.0078125) - 3.6927934 * jax.random.uniform(arg_keys[4], (VIEWS, TOF_BINS, NX), jnp.float32) ** block_levels(arg_keys[4], (VIEWS, TOF_BINS, NX), ((0, 8),), -0.2, 0.2)), 0.00019454956, 0.0078125).astype(jnp.bfloat16)
    axial_mix = draw_axial_mix(jax.random.fold_in(arg_keys[8], 71), 0)
    background = jnp.clip(jnp.exp(math.log(2.0) - 1.3862944 * jax.random.uniform(arg_keys[6], (VIEWS, TOF_BINS, NY, SLICES), jnp.float32) ** block_levels(arg_keys[6], (VIEWS, TOF_BINS, NY, SLICES), ((0, 8), (2, 32)), -0.2, 0.2)), 0.5, 2.0)
    counts = set_ends(jax.random.randint(arg_keys[7], (VIEWS, TOF_BINS, NY, SLICES), 0, 20), jax.random.fold_in(arg_keys[7], 1), 0, 19).astype(jnp.int32)
    return dict(image=image, sensitivity=sensitivity, resample_x=resample_x, resample_y=resample_y, tof_kernel=tof_kernel, axial_mix=axial_mix, background=background, counts=counts)


def one_view(image_low, resample_xv, resample_yv, tof_v, mix_v, background_v, counts_v):
    hi = lax.Precision.HIGHEST
    along_y = jnp.einsum("zxy,yb->zxb", image_low.astype(jnp.float32), resample_yv.astype(jnp.float32)).astype(jnp.bfloat16)
    rotated = jnp.einsum("zxb,ax->zba", along_y.astype(jnp.float32), resample_xv.astype(jnp.float32)).astype(jnp.bfloat16)
    integrals = jnp.einsum("ka,zba->kbz", tof_v.astype(jnp.float32), rotated.astype(jnp.float32))
    expected = background_v + jnp.einsum("kbz,cz->kbc", integrals, mix_v, precision=hi)
    ratios = counts_v.astype(jnp.float32) / expected
    back_mixed = jnp.einsum("kbc,cz->kbz", ratios, mix_v, precision=hi).astype(jnp.bfloat16)
    frames = jnp.einsum("ka,kbz->zba", tof_v.astype(jnp.float32), back_mixed.astype(jnp.float32)).astype(jnp.bfloat16)
    unrotated = jnp.einsum("zba,yb->zya", frames.astype(jnp.float32), resample_yv.astype(jnp.float32)).astype(jnp.bfloat16)
    return jnp.einsum("zya,ax->zxy", unrotated.astype(jnp.float32), resample_xv.astype(jnp.float32))


def reference(image, sensitivity, resample_x, resample_y, tof_kernel, axial_mix, background, counts):
    image_low = image.astype(jnp.bfloat16)

    def accumulate(carry, inputs):
        resample_xv, resample_yv, tof_v, mix_v, background_v, counts_v = inputs
        return carry + one_view(image_low, resample_xv, resample_yv, tof_v, mix_v, background_v, counts_v), None

    start_sum = jnp.zeros(image.shape, jnp.float32)
    gradient, unused = lax.scan(accumulate, start_sum, (resample_x, resample_y, tof_kernel, axial_mix, background, counts))
    return image * gradient / sensitivity
```

```python
import jax
import jax.numpy as jnp
from jax import lax
from jax.sharding import PartitionSpec as P


def local(image, sensitivity, resample_x, resample_y, tof_kernel, axial_mix, background, counts):
    highest = lax.Precision.HIGHEST
    image_low = image.astype(jnp.bfloat16)
    along_y = jnp.einsum(
        "zxy,vyb->vzxb", image_low, resample_y, preferred_element_type=jnp.float32
    ).astype(jnp.bfloat16)
    rotated = jnp.einsum(
        "vzxb,vax->vzba", along_y, resample_x, preferred_element_type=jnp.float32
    ).astype(jnp.bfloat16)
    views, own, bins, _ = rotated.shape
    tof = tof_kernel.shape[1]
    integrals = jnp.einsum(
        "vka,vzba->bvzk", tof_kernel, rotated, preferred_element_type=jnp.float32
    )
    parts = lax.axis_size("slab")
    gathered = lax.all_to_all(
        integrals.reshape(parts, bins // parts, views * own * tof), "slab", split_axis=0, concat_axis=0, tiled=True
    ).reshape(parts, bins // parts, views, own, tof)
    gathered = jnp.transpose(gathered, (2, 4, 1, 0, 3)).reshape(views, tof, bins // parts, parts * own)
    expected = background + jnp.einsum("vkbz,vcz->vkbc", gathered, axial_mix, precision=highest)
    ratios = counts.astype(jnp.float32) / expected
    back_mixed = jnp.einsum("vkbc,vcz->vkbz", ratios, axial_mix, precision=highest).astype(
        jnp.bfloat16
    )
    back_mixed = jnp.transpose(back_mixed.reshape(views, tof, bins // parts, parts, own), (3, 2, 0, 4, 1))
    back_mixed = lax.all_to_all(
        back_mixed.reshape(parts, bins // parts, views * own * tof), "slab", split_axis=0, concat_axis=0, tiled=True
    ).reshape(bins, views, own, tof)
    frames = jnp.einsum(
        "vka,bvzk->vzba", tof_kernel, back_mixed, preferred_element_type=jnp.float32
    ).astype(jnp.bfloat16)
    unrotated = jnp.einsum(
        "vzba,vyb->vzya", frames, resample_y, preferred_element_type=jnp.float32
    ).astype(jnp.bfloat16)
    own_rows = image.shape[1] // lax.axis_size("view")
    gradient = lax.psum_scatter(
        jnp.einsum("vzya,vax->xzy", unrotated, resample_x, preferred_element_type=jnp.float32),
        "view",
        scatter_dimension=0,
        tiled=True,
    )
    gradient = jnp.transpose(gradient, (1, 0, 2))
    current = lax.dynamic_slice_in_dim(image, lax.axis_index("view") * own_rows, own_rows, 1)
    return current * gradient / sensitivity


def solution(mesh):
    in_specs = (
        P("slab", None, None),
        P("slab", "view", None),
        P("view", None, None),
        P("view", None, None),
        P("view", None, None),
        P("view", None, None),
        P("view", None, "slab", None),
        P("view", None, "slab", None),
    )
    out_specs = P("slab", "view", None)
    return jax.shard_map(local, mesh=mesh, in_specs=in_specs, out_specs=out_specs, check_vma=False)
```

```python
import functools

import jax
import jax.numpy as jnp
from jax import lax
from jax.experimental import pallas as pl
from jax.experimental.pallas import tpu as pltpu
from jax.sharding import PartitionSpec as P

F32, BF16 = jnp.float32, jnp.bfloat16
MESH = pl.DeviceIdType.MESH
LEVELS = 32767.0


def dot(a, b, transposed=False):
    dims = (((1,), (1 if transposed else 0,)), ((), ()))
    return lax.dot_general(a, b, dims, preferred_element_type=F32)


def forward_kernel(image_ref, rx_ref, ry_ref, tof_ref, out_ref, sums):
    z = pl.program_id(0)
    views, tof = tof_ref.shape[0], tof_ref.shape[1]
    low = image_ref[0].astype(BF16)
    for v in range(views):
        along_y = dot(low, ry_ref[v]).astype(BF16)
        rotated = dot(rx_ref[v], along_y).astype(BF16)
        row = pl.multiple_of((z * views + v) * tof, tof)
        sums[pl.ds(row, tof), :] = dot(tof_ref[v], rotated)

    @pl.when(z == pl.num_programs(0) - 1)
    def _():
        out_ref[...] = sums[...].T


def forward(image, rx, ry, tof):
    own, nx, ny = image.shape
    lanes = own * tof.shape[0] * tof.shape[1]
    whole = lambda a: pl.BlockSpec(a.shape, lambda z: (0,) * a.ndim)
    return pl.pallas_call(
        forward_kernel,
        grid=(own,),
        out_shape=jax.ShapeDtypeStruct((ny, lanes), F32),
        in_specs=[pl.BlockSpec((1, nx, ny), lambda z: (z, 0, 0)), whole(rx), whole(ry), whole(tof)],
        out_specs=pl.BlockSpec((ny, lanes), lambda z: (0, 0)),
        scratch_shapes=[pltpu.VMEM((lanes, ny), F32)],
        compiler_params=pltpu.CompilerParams(vmem_limit_bytes=48 << 20),
        name="forward",
    )(image, rx, ry, tof)


def split(a):
    high = a.astype(BF16)
    return high, (a - high.astype(F32)).astype(BF16)


def three(a, b):
    (ah, al), (bh, bl) = a, b
    return dot(ah, bh) + (dot(al, bh) + dot(ah, bl))


def mix_kernel(
    sums_ref, mix_ref, mix_t_ref, background_ref, counts_ref, out_ref,
    arrived, back, wide, given, counted, staged, send_sem, recv_sem, back_send, back_recv,
):
    parts, bins, lanes = arrived.shape
    me = lax.axis_index("slab")
    barrier = pltpu.get_barrier_semaphore()

    def greet(o, carry):
        peer = lax.rem(me + o, parts)
        pl.semaphore_signal(barrier, inc=1, device_id={"slab": peer}, device_id_type=MESH)
        return carry

    lax.fori_loop(1, parts, greet, 0)
    rows = lanes // 4
    for b in range(bins):
        held = background_ref[pl.ds(b, rows, stride=bins), :]
        given[:, b * lanes:(b + 1) * lanes] = jnp.concatenate([held] * 4, axis=0).T
        held = counts_ref[pl.ds(b, rows, stride=bins), :].astype(F32)
        counted[:, b * lanes:(b + 1) * lanes] = jnp.concatenate([held] * 4, axis=0).T
    pl.semaphore_wait(barrier, parts - 1)

    def block(ref, i):
        return ref.at[pl.ds(pl.multiple_of(i * bins, bins), bins), :]

    def send(o, carry):
        peer = lax.rem(me + o, parts)
        pltpu.make_async_remote_copy(
            src_ref=block(sums_ref, peer), dst_ref=arrived.at[me], send_sem=send_sem, recv_sem=recv_sem,
            device_id={"slab": peer}, device_id_type=MESH,
        ).start()
        return carry

    lax.fori_loop(1, parts, send, 0)
    arrived[me] = block(sums_ref, me)[...]
    most = pltpu.make_async_remote_copy(
        src_ref=arrived.at[pl.ds(0, parts - 1)], dst_ref=arrived.at[pl.ds(0, parts - 1)],
        send_sem=send_sem, recv_sem=recv_sem, device_id={"slab": me}, device_id_type=MESH,
    )
    most.wait_recv()

    depth = mix_ref.shape[1]
    row = lax.broadcasted_iota(jnp.int32, (depth, lanes), 0) // parts
    lane = lax.broadcasted_iota(jnp.int32, (depth, lanes), 1)
    views = depth // (4 * parts)
    tof = rows // views
    mine = row == (lane % rows // tof) * 4 + lane // rows
    for b in range(bins):
        held = arrived[:, b, :]
        wide[:, b * lanes:(b + 1) * lanes] = jnp.where(mine, jnp.concatenate([held] * (depth // parts), axis=0), 0.0)
    mixes = split(mix_ref[...])
    mixes_t = split(mix_t_ref[...])
    step = 2 * lanes
    for b in range(0, bins, 2):
        at = slice(b * lanes, b * lanes + step)
        total = three(mixes, split(wide[:, at]))
        ratios = []
        for h in range(2):
            one = total[:, h * lanes:(h + 1) * lanes]
            one = one + pltpu.roll(one, 2 * rows, 1)
            one = one + pltpu.roll(one, rows, 1)
            inner = slice((b + h) * lanes, (b + h + 1) * lanes)
            ratios.append(counted[:, inner] / (given[:, inner] + one))
        ratios = jnp.concatenate(ratios, axis=1)
        spread = three(mixes_t, split(ratios))
        for h in range(2):
            one = jnp.where(mine, spread[:, h * lanes:(h + 1) * lanes], 0.0)
            held = one[:parts]
            for g in range(1, depth // parts):
                held = held + one[g * parts:(g + 1) * parts]
            staged[pl.ds(b + h, parts, stride=bins), :] = held
    back[...] = staged[...].astype(BF16)

    def send_back(o, carry):
        peer = lax.rem(me + o, parts)
        pltpu.make_async_remote_copy(
            src_ref=block(back, peer), dst_ref=block(out_ref, me), send_sem=back_send, recv_sem=back_recv,
            device_id={"slab": peer}, device_id_type=MESH,
        ).start()
        return carry

    lax.fori_loop(1, parts, send_back, 0)
    block(out_ref, me)[...] = block(back, me)[...]
    few = pl.ds(0, (parts - 1) * bins)
    rest = pltpu.make_async_remote_copy(
        src_ref=back.at[few, :], dst_ref=out_ref.at[few, :],
        send_sem=back_send, recv_sem=back_recv, device_id={"slab": me}, device_id_type=MESH,
    )
    rest.wait_recv()
    most.wait_send()
    rest.wait_send()


def mix_slices(sums, mix, background, counts):
    parts = lax.axis_size("slab")
    rows, lanes = sums.shape
    bins = rows // parts
    views, planes, slices = mix.shape
    own = slices // parts
    mix_t = jnp.transpose(mix.reshape(views, planes, parts, own), (0, 3, 2, 1)).reshape(views * slices, planes)
    flat = background.shape[0] * background.shape[1] * background.shape[2]
    vmem = pl.BlockSpec(memory_space=pltpu.VMEM)
    return pl.pallas_call(
        mix_kernel,
        out_shape=jax.ShapeDtypeStruct((rows, lanes), BF16),
        in_specs=[vmem] * 5,
        out_specs=vmem,
        scratch_shapes=[
            pltpu.VMEM((parts, bins, lanes), F32),
            pltpu.VMEM((rows, lanes), BF16),
            pltpu.VMEM((views * slices, bins * lanes), F32),
            pltpu.VMEM((planes, bins * lanes), F32),
            pltpu.VMEM((planes, bins * lanes), F32),
            pltpu.VMEM((rows, lanes), F32),
            pltpu.SemaphoreType.DMA,
            pltpu.SemaphoreType.DMA,
            pltpu.SemaphoreType.DMA,
            pltpu.SemaphoreType.DMA,
        ],
        compiler_params=pltpu.CompilerParams(collective_id=0, has_side_effects=True, vmem_limit_bytes=48 << 20),
        name="mix_slices",
    )(sums, mix_t.T, mix_t, background.reshape(flat, planes), counts.reshape(flat, planes))


def back_kernel(
    back_ref, image_ref, sensitivity_ref, rx_ref, ry_ref, tof_ref, out_ref,
    rx_t, tof_wide, partial, other, codes, scales, codes_in, scales_in, current,
    load_sem, pair_send, pair_recv, code_send, code_recv, scale_send, scale_recv,
):
    me = lax.axis_index("view")
    core, chip = me % 2, me // 2
    own, own_rows = sensitivity_ref.shape[0], sensitivity_ref.shape[1]
    views, tof = tof_ref.shape[0], tof_ref.shape[1]
    lanes = back_ref.shape[1]
    nx = rx_ref.shape[2]
    half = nx // 2
    chips = half // own_rows
    barrier = pltpu.get_barrier_semaphore()
    peers = [me + 1 - 2 * core] + [lax.rem(chip + o, chips) * 2 + core for o in range(1, chips)]
    for peer in peers:
        pl.semaphore_signal(barrier, inc=1, device_id={"view": peer}, device_id_type=MESH)
    load = pltpu.make_async_copy(
        image_ref.at[:, pl.ds(pl.multiple_of(me * own_rows, own_rows), own_rows), :], current, load_sem
    )
    load.start()
    for v in range(views):
        turned = rx_ref[v].T
        for c in range(2):
            for x in range(chips):
                rx_t[v, (c * chips + x) * own_rows:(c * chips + x + 1) * own_rows, :] = (
                    turned[(2 * x + c) * own_rows:(2 * x + c + 1) * own_rows]
                )
    tof_wide[...] = jnp.zeros_like(tof_wide)
    for z in range(own):
        for v in range(views):
            at = (z * views + v) * tof
            tof_wide[z * views + v, at:at + tof, :] = tof_ref[v]

    def ours(which):
        return pl.ds(pl.multiple_of(which * half, half), half)

    def pair(z):
        return pltpu.make_async_remote_copy(
            src_ref=partial.at[z, ours(1 - core), :], dst_ref=other.at[z],
            send_sem=pair_send.at[z], recv_sem=pair_recv.at[z], device_id={"view": peers[0]}, device_id_type=MESH,
        )

    def leg(z, o):
        data = pltpu.make_async_remote_copy(
            src_ref=codes.at[z, o - 1], dst_ref=codes_in.at[z, o - 1],
            send_sem=code_send.at[z, o - 1], recv_sem=code_recv.at[z, o - 1],
            device_id={"view": peers[o]}, device_id_type=MESH,
        )
        scale = pltpu.make_async_remote_copy(
            src_ref=scales.at[z, o - 1], dst_ref=scales_in.at[z, o - 1],
            send_sem=scale_send.at[z, o - 1], recv_sem=scale_recv.at[z, o - 1],
            device_id={"view": peers[o]}, device_id_type=MESH,
        )
        return data, scale

    def rows_of(o):
        at = pl.multiple_of(lax.rem(chip + o, chips) * own_rows, own_rows)
        return pl.ds(at, own_rows), pl.ds(pl.multiple_of(core * half + at, own_rows), own_rows)

    def project(z):
        total = None
        for v in range(views):
            frames = dot(back_ref[...], tof_wide[z * views + v]).astype(BF16)
            unrotated = dot(ry_ref[v], frames).astype(BF16)
            term = dot(rx_t[v], unrotated, transposed=True)
            total = term if total is None else total + term
        partial[z] = total

    def onward(z):
        pair(z).wait_recv()
        for o in (2, 1, 3):
            theirs, mine = rows_of(o)
            block = partial[z, mine, :] + other[z, theirs, :]
            top = jnp.maximum(jnp.max(jnp.abs(block), axis=0, keepdims=True), 1e-30)
            codes[z, o - 1] = jnp.round(block * (LEVELS / top)).astype(jnp.int32).astype(jnp.int16)
            scales[z, o - 1] = jnp.broadcast_to(top * (1.0 / LEVELS), scales.shape[2:])
            for copy in leg(z, o):
                copy.start()

    for z in range(own):
        project(z)
        if z == 0:
            pl.semaphore_wait(barrier, len(peers))
        pair(z).start()
        if z > 0:
            onward(z - 1)
    onward(own - 1)
    load.wait()
    for z in range(own):
        theirs, mine = rows_of(0)
        total = partial[z, mine, :] + other[z, theirs, :]
        for o in (1, 3, 2):
            for copy in leg(z, o):
                copy.wait_recv()
            total = total + codes_in[z, o - 1].astype(jnp.int32).astype(F32) * scales_in[z, o - 1][:1]
        out_ref[z] = current[z] * total / sensitivity_ref[z]
    for z in range(own):
        pair(z).wait_send()
        for o in range(1, chips):
            for copy in leg(z, o):
                copy.wait_send()


def project_back(back, image, sensitivity, rx, ry, tof):
    own, own_rows, ny = sensitivity.shape
    views, bins, nx = tof.shape
    half = nx // 2
    others = half // own_rows - 1
    vmem = pl.BlockSpec(memory_space=pltpu.VMEM)
    dma = pltpu.SemaphoreType.DMA
    return pl.pallas_call(
        back_kernel,
        out_shape=jax.ShapeDtypeStruct(sensitivity.shape, F32),
        in_specs=[vmem, pl.BlockSpec(memory_space=pl.ANY)] + [vmem] * 4,
        out_specs=vmem,
        scratch_shapes=[
            pltpu.VMEM((views, nx, nx), BF16),
            pltpu.VMEM((own * views, back.shape[1], nx), BF16),
            pltpu.VMEM((own, nx, ny), F32),
            pltpu.VMEM((own, half, ny), F32),
            pltpu.VMEM((own, others, own_rows, ny), jnp.int16),
            pltpu.VMEM((own, others, 8, ny), F32),
            pltpu.VMEM((own, others, own_rows, ny), jnp.int16),
            pltpu.VMEM((own, others, 8, ny), F32),
            pltpu.VMEM((own, own_rows, ny), F32),
            dma,
            dma((own,)), dma((own,)),
            dma((own, others)), dma((own, others)), dma((own, others)), dma((own, others)),
        ],
        compiler_params=pltpu.CompilerParams(collective_id=1, has_side_effects=True, vmem_limit_bytes=48 << 20),
        name="project_back",
    )(back, image, sensitivity, rx, ry, tof)


def local(image, sensitivity, resample_x, resample_y, tof_kernel, axial_mix, background, counts):
    sums = forward(image, resample_x, resample_y, tof_kernel)
    back = mix_slices(sums, axial_mix, background, counts)
    return project_back(back, image, sensitivity, resample_x, resample_y, tof_kernel)


def solution(mesh):
    in_specs = (
        P("slab", None, None),
        P("slab", "view", None),
        P("view", None, None),
        P("view", None, None),
        P("view", None, None),
        P("view", None, None),
        P("view", None, "slab", None),
        P("view", None, "slab", None),
    )
    out_specs = P("slab", "view", None)
    return jax.shard_map(local, mesh=mesh, in_specs=in_specs, out_specs=out_specs, check_vma=False)
```

```python
import jax
import jax.numpy as jnp
from jax import lax
from jax.experimental import pallas as pl
from jax.experimental.pallas import tpu as pltpu
from jax.sharding import PartitionSpec as P

F32, BF16 = jnp.float32, jnp.bfloat16
MESH = pl.DeviceIdType.MESH
LEVELS = 32767.0


def dot(a, b, transposed=False):
    dims = (((1,), (1 if transposed else 0,)), ((), ()))
    return lax.dot_general(a, b, dims, preferred_element_type=F32)


def split(a):
    high = a.astype(BF16)
    return high, (a - high.astype(F32)).astype(BF16)


def kernel(
    image_hbm, sens_hbm, rx_hbm, ry_hbm, tof_hbm, mix_hbm, background_hbm, counts_hbm, out_ref,
    image, sens, rx, ry, tof_ref, mix, background, counts, current,
    sums, sending, arrived, back, back_in, wide, given, counted, staged, mix_t, mix_rows,
    rx_t, tof_wide, partial, other, codes, scales, codes_in, scales_in,
    load_sem, send_sem, recv_sem, back_send, back_recv,
    pair_send, pair_recv, code_send, code_recv, scale_send, scale_recv,
):
    own, own_rows = sens.shape[0], sens.shape[1]
    views, tof = tof_ref.shape[0], tof_ref.shape[1]
    parts, bins, lanes = arrived.shape
    nx = rx.shape[2]
    half = nx // 2
    chips = half // own_rows
    rows = views * tof
    planes = mix.shape[2]
    depth = views * own * parts
    slab = lax.axis_index("slab")
    me = lax.axis_index("view")
    core, chip = me % 2, me // 2

    loads = [
        pltpu.make_async_copy(image_hbm.at[0], image.at[0], load_sem.at[0]),
        pltpu.make_async_copy(ry_hbm, ry, load_sem.at[1]),
        pltpu.make_async_copy(rx_hbm, rx, load_sem.at[2]),
        pltpu.make_async_copy(tof_hbm, tof_ref, load_sem.at[3]),
    ]
    loads += [pltpu.make_async_copy(image_hbm.at[z], image.at[z], load_sem.at[3 + z]) for z in range(1, own)]
    late = [
        pltpu.make_async_copy(mix_hbm, mix, load_sem.at[own + 3]),
        pltpu.make_async_copy(background_hbm, background, load_sem.at[own + 4]),
        pltpu.make_async_copy(counts_hbm, counts, load_sem.at[own + 5]),
        pltpu.make_async_copy(sens_hbm, sens, load_sem.at[own + 6]),
        pltpu.make_async_copy(
            image_hbm.at[:, pl.ds(pl.multiple_of(me * own_rows, own_rows), own_rows), :], current, load_sem.at[own + 7]
        ),
    ]
    for copy in loads + late:
        copy.start()

    barrier = pltpu.get_barrier_semaphore()

    def greet(o, carry):
        peer = lax.rem(slab + o, parts)
        pl.semaphore_signal(barrier, inc=1, device_id={"slab": peer}, device_id_type=MESH)
        return carry

    lax.fori_loop(1, parts, greet, 0)
    peers = [me + 1 - 2 * core] + [lax.rem(chip + o, chips) * 2 + core for o in range(1, chips)]
    for peer in peers:
        pl.semaphore_signal(barrier, inc=1, device_id={"view": peer}, device_id_type=MESH)

    for z in range(own):
        if z == 0:
            for copy in loads[:4]:
                copy.wait()
        else:
            loads[3 + z].wait()
        low = image[z].astype(BF16)
        for v in range(views):
            along_y = dot(low, ry[v]).astype(BF16)
            rotated = dot(rx[v], along_y).astype(BF16)
            at = (z * views + v) * tof
            sums[at:at + tof, :] = dot(tof_ref[v], rotated)
    sending[...] = sums[...].T.astype(BF16)

    def block(ref, i):
        return ref.at[pl.ds(pl.multiple_of(i * bins, bins), bins), :]

    def send(o, carry):
        peer = lax.rem(slab + o, parts)
        pltpu.make_async_remote_copy(
            src_ref=block(sending, peer), dst_ref=arrived.at[slab], send_sem=send_sem, recv_sem=recv_sem,
            device_id={"slab": peer}, device_id_type=MESH,
        ).start()
        return carry

    pl.semaphore_wait(barrier, parts - 1 + len(peers))
    lax.fori_loop(1, parts, send, 0)
    arrived[slab] = block(sending, slab)[...]

    for copy in late:
        copy.wait()
    for b in range(bins):
        held = background[pl.ds(b, rows, stride=bins), :]
        given[:, b * lanes:(b + 1) * lanes] = jnp.concatenate([held] * own, axis=0).T
        held = counts[pl.ds(b, rows, stride=bins), :].astype(F32)
        counted[:, b * lanes:(b + 1) * lanes] = jnp.concatenate([held] * own, axis=0).T
    slices = own * parts
    for v in range(views):
        mix_rows[v * slices:(v + 1) * slices, :] = mix[v].T
    for v in range(views):
        for z in range(own):
            at = (v * own + z) * parts
            mix_t[at:at + parts, :] = mix_rows[pl.ds(v * slices + z, parts, stride=own), :]
    mixes_t = split(mix_t[...])
    mixes = split(mix_t[...].T)
    for v in range(views):
        turned = rx[v].T
        for c in range(2):
            for x in range(chips):
                rx_t[v, (c * chips + x) * own_rows:(c * chips + x + 1) * own_rows, :] = (
                    turned[(2 * x + c) * own_rows:(2 * x + c + 1) * own_rows]
                )
    tof_wide[...] = jnp.zeros_like(tof_wide)
    for z in range(own):
        for v in range(views):
            at = (z * views + v) * tof
            tof_wide[z * views + v, at:at + tof, :] = tof_ref[v]

    most = pltpu.make_async_remote_copy(
        src_ref=arrived.at[pl.ds(0, parts - 1)], dst_ref=arrived.at[pl.ds(0, parts - 1)],
        send_sem=send_sem, recv_sem=recv_sem, device_id={"slab": slab}, device_id_type=MESH,
    )
    most.wait_recv()

    row = lax.broadcasted_iota(jnp.int32, (depth, lanes), 0) // parts
    lane = lax.broadcasted_iota(jnp.int32, (depth, lanes), 1)
    mine = row == (lane % rows // tof) * own + lane // rows
    staged[...] = arrived[...].astype(F32).reshape(staged.shape)
    for b in range(bins):
        held = staged[pl.ds(b, parts, stride=bins), :]
        held = jnp.where(mine, jnp.concatenate([held] * (depth // parts), axis=0), 0.0)
        wide[:, b * lanes:(b + 1) * lanes] = held.astype(BF16)
    step = 2 * lanes
    for b in range(0, bins, 2):
        at = slice(b * lanes, b * lanes + step)
        total = dot(mixes[0], wide[:, at]) + dot(mixes[1], wide[:, at])
        ratios = []
        for h in range(2):
            one = total[:, h * lanes:(h + 1) * lanes]
            one = one + pltpu.roll(one, 2 * rows, 1)
            one = one + pltpu.roll(one, rows, 1)
            inner = slice((b + h) * lanes, (b + h + 1) * lanes)
            ratios.append(counted[:, inner] / (given[:, inner] + one))
        high, low = split(jnp.concatenate(ratios, axis=1))
        spread = dot(mixes_t[0], high) + (dot(mixes_t[1], high) + dot(mixes_t[0], low))
        for h in range(2):
            one = jnp.where(mine, spread[:, h * lanes:(h + 1) * lanes], 0.0)
            held = one[:parts]
            for g in range(1, depth // parts):
                held = held + one[g * parts:(g + 1) * parts]
            staged[pl.ds(b + h, parts, stride=bins), :] = held
    back[...] = staged[...].astype(BF16)

    def send_back(o, carry):
        peer = lax.rem(slab + o, parts)
        pltpu.make_async_remote_copy(
            src_ref=block(back, peer), dst_ref=block(back_in, slab), send_sem=back_send, recv_sem=back_recv,
            device_id={"slab": peer}, device_id_type=MESH,
        ).start()
        return carry

    lax.fori_loop(1, parts, send_back, 0)
    block(back_in, slab)[...] = block(back, slab)[...]
    few = pl.ds(0, (parts - 1) * bins)
    rest = pltpu.make_async_remote_copy(
        src_ref=back.at[few, :], dst_ref=back_in.at[few, :],
        send_sem=back_send, recv_sem=back_recv, device_id={"slab": slab}, device_id_type=MESH,
    )
    rest.wait_recv()

    def ours(which):
        return pl.ds(pl.multiple_of(which * half, half), half)

    def pair(z):
        return pltpu.make_async_remote_copy(
            src_ref=partial.at[z, ours(1 - core), :], dst_ref=other.at[z],
            send_sem=pair_send.at[z], recv_sem=pair_recv.at[z], device_id={"view": peers[0]}, device_id_type=MESH,
        )

    def leg(z, o):
        data = pltpu.make_async_remote_copy(
            src_ref=codes.at[z, o - 1], dst_ref=codes_in.at[z, o - 1],
            send_sem=code_send.at[z, o - 1], recv_sem=code_recv.at[z, o - 1],
            device_id={"view": peers[o]}, device_id_type=MESH,
        )
        scale = pltpu.make_async_remote_copy(
            src_ref=scales.at[z, o - 1], dst_ref=scales_in.at[z, o - 1],
            send_sem=scale_send.at[z, o - 1], recv_sem=scale_recv.at[z, o - 1],
            device_id={"view": peers[o]}, device_id_type=MESH,
        )
        return data, scale

    def rows_of(o):
        at = pl.multiple_of(lax.rem(chip + o, chips) * own_rows, own_rows)
        return pl.ds(at, own_rows), pl.ds(pl.multiple_of(core * half + at, own_rows), own_rows)

    def project(z):
        total = None
        for v in range(views):
            frames = dot(back_in[...], tof_wide[z * views + v]).astype(BF16)
            unrotated = dot(ry[v], frames).astype(BF16)
            term = dot(rx_t[v], unrotated, transposed=True)
            total = term if total is None else total + term
        partial[z] = total

    def onward(z):
        pair(z).wait_recv()
        for o in (2, 1, 3):
            theirs, ours_at = rows_of(o)
            held = partial[z, ours_at, :] + other[z, theirs, :]
            top = jnp.maximum(jnp.max(jnp.abs(held), axis=0, keepdims=True), 1e-30)
            codes[z, o - 1] = jnp.round(held * (LEVELS / top)).astype(jnp.int32).astype(jnp.int16)
            scales[z, o - 1] = top * (1.0 / LEVELS)
            for copy in leg(z, o):
                copy.start()

    for z in range(own):
        project(z)
        pair(z).start()
        if z > 0:
            onward(z - 1)
    onward(own - 1)
    for z in range(own):
        theirs, ours_at = rows_of(0)
        total = partial[z, ours_at, :] + other[z, theirs, :]
        for o in (1, 3, 2):
            for copy in leg(z, o):
                copy.wait_recv()
            total = total + codes_in[z, o - 1].astype(jnp.int32).astype(F32) * scales_in[z, o - 1]
        out_ref[z] = current[z] * total / sens[z]
    most.wait_send()
    rest.wait_send()
    for z in range(own):
        pair(z).wait_send()
        for o in range(1, chips):
            for copy in leg(z, o):
                copy.wait_send()


def local(image, sensitivity, resample_x, resample_y, tof_kernel, axial_mix, background, counts):
    parts = lax.axis_size("slab")
    own, own_rows, ny = sensitivity.shape
    views, tof, nx = tof_kernel.shape
    bins, planes = background.shape[2:]
    lanes = own * views * tof
    half = nx // 2
    others = half // own_rows - 1
    flat = views * tof * bins
    vm, dma, i32, i16 = pltpu.VMEM, pltpu.SemaphoreType.DMA, jnp.int32, jnp.int16
    hbm = pl.BlockSpec(memory_space=pl.ANY)
    return pl.pallas_call(
        kernel,
        out_shape=jax.ShapeDtypeStruct(sensitivity.shape, F32),
        in_specs=[hbm] * 8,
        out_specs=pl.BlockSpec(memory_space=pltpu.VMEM),
        scratch_shapes=[
            vm(image.shape, F32), vm(sensitivity.shape, F32),
            vm(resample_x.shape, BF16), vm(resample_y.shape, BF16), vm(tof_kernel.shape, BF16),
            vm(axial_mix.shape, F32), vm((flat, planes), F32), vm((flat, planes), i32),
            vm(sensitivity.shape, F32),
            vm((lanes, ny), F32), vm((ny, lanes), BF16), vm((parts, bins, lanes), BF16),
            vm((ny, lanes), BF16), vm((ny, lanes), BF16),
            vm((views * own * parts, bins * lanes), BF16),
            vm((planes, bins * lanes), F32), vm((planes, bins * lanes), F32),
            vm((ny, lanes), F32),
            vm((views * own * parts, planes), F32), vm((views * own * parts, planes), F32),
            vm((views, nx, nx), BF16), vm((own * views, lanes, nx), BF16),
            vm((own, nx, ny), F32), vm((own, half, ny), F32),
            vm((own, others, own_rows, ny), i16), vm((own, others, 1, ny), F32),
            vm((own, others, own_rows, ny), i16), vm((own, others, 1, ny), F32),
            dma((own + 8,)), dma, dma, dma, dma,
            dma((own,)), dma((own,)),
            dma((own, others)), dma((own, others)), dma((own, others)), dma((own, others)),
        ],
        compiler_params=pltpu.CompilerParams(collective_id=0, has_side_effects=True, vmem_limit_bytes=56 << 20),
        name="update",
    )(
        image, sensitivity, resample_x, resample_y, tof_kernel, axial_mix,
        background.reshape(flat, planes), counts.reshape(flat, planes),
    )


def solution(mesh):
    in_specs = (
        P("slab", None, None),
        P("slab", "view", None),
        P("view", None, None),
        P("view", None, None),
        P("view", None, None),
        P("view", None, None),
        P("view", None, "slab", None),
        P("view", None, "slab", None),
    )
    out_specs = P("slab", "view", None)
    return jax.shard_map(local, mesh=mesh, in_specs=in_specs, out_specs=out_specs, check_vma=False)
```

```python
import jax
import jax.numpy as jnp
from jax import lax
from jax.experimental import pallas as pl
from jax.experimental.pallas import tpu as pltpu
from jax.sharding import PartitionSpec as P

F32, BF16 = jnp.float32, jnp.bfloat16
MESH = pl.DeviceIdType.MESH
LEVELS = 32767.0


def dot(a, b, transposed=False):
    dims = (((1,), (1 if transposed else 0,)), ((), ()))
    return lax.dot_general(a, b, dims, preferred_element_type=F32)


def split(a):
    high = a.astype(BF16)
    return high, (a - high.astype(F32)).astype(BF16)


def kernel(
    image_hbm, sens_hbm, rx_hbm, ry_hbm, tof_hbm, mix_hbm, background_hbm, counts_hbm, out_ref,
    image, sens, rx, ry, tof_ref, mix, background, counts, current,
    sums, sending, arrived, back, back_in, wide, given, counted, staged, mix_t, mix_rows,
    rx_t, tof_wide, partial, other, codes, scales, codes_in, scales_in,
    load_sem, send_sem, recv_sem, back_send, back_recv,
    pair_send, pair_recv, code_send, code_recv, scale_send, scale_recv,
):
    own, own_rows = sens.shape[0], sens.shape[1]
    views, tof = tof_ref.shape[0], tof_ref.shape[1]
    parts, bins, lanes = arrived.shape
    nx = rx.shape[2]
    half = nx // 2
    chips = half // own_rows
    rows = views * tof
    planes = mix.shape[2]
    slab = lax.axis_index("slab")
    me = lax.axis_index("view")
    core, chip = me % 2, me // 2

    loads = [
        pltpu.make_async_copy(image_hbm.at[0], image.at[0], load_sem.at[0]),
        pltpu.make_async_copy(ry_hbm, ry, load_sem.at[1]),
        pltpu.make_async_copy(rx_hbm, rx, load_sem.at[2]),
        pltpu.make_async_copy(tof_hbm, tof_ref, load_sem.at[3]),
    ]
    loads += [pltpu.make_async_copy(image_hbm.at[z], image.at[z], load_sem.at[3 + z]) for z in range(1, own)]
    late = [
        pltpu.make_async_copy(mix_hbm, mix, load_sem.at[own + 3]),
        pltpu.make_async_copy(background_hbm, background, load_sem.at[own + 4]),
        pltpu.make_async_copy(counts_hbm, counts, load_sem.at[own + 5]),
        pltpu.make_async_copy(sens_hbm, sens, load_sem.at[own + 6]),
        pltpu.make_async_copy(
            image_hbm.at[:, pl.ds(pl.multiple_of(me * own_rows, own_rows), own_rows), :], current, load_sem.at[own + 7]
        ),
    ]
    for copy in loads + late:
        copy.start()

    barrier = pltpu.get_barrier_semaphore()

    def greet(o, carry):
        peer = lax.rem(slab + o, parts)
        pl.semaphore_signal(barrier, inc=1, device_id={"slab": peer}, device_id_type=MESH)
        return carry

    lax.fori_loop(1, parts, greet, 0)
    peers = [me + 1 - 2 * core] + [lax.rem(chip + o, chips) * 2 + core for o in range(1, chips)]
    for peer in peers:
        pl.semaphore_signal(barrier, inc=1, device_id={"view": peer}, device_id_type=MESH)

    for z in range(own):
        if z == 0:
            for copy in loads[:4]:
                copy.wait()
        else:
            loads[3 + z].wait()
        low = image[z].astype(BF16)
        for v in range(views):
            along_y = dot(low, ry[v]).astype(BF16)
            rotated = dot(rx[v], along_y).astype(BF16)
            at = (z * views + v) * tof
            sums[at:at + tof, :] = dot(tof_ref[v], rotated)
    sending[...] = sums[...].T.astype(BF16)

    def block(ref, i):
        return ref.at[pl.ds(pl.multiple_of(i * bins, bins), bins), :]

    def send(o, carry):
        peer = lax.rem(slab + o, parts)
        pltpu.make_async_remote_copy(
            src_ref=block(sending, peer), dst_ref=arrived.at[slab], send_sem=send_sem, recv_sem=recv_sem,
            device_id={"slab": peer}, device_id_type=MESH,
        ).start()
        return carry

    pl.semaphore_wait(barrier, parts - 1 + len(peers))
    lax.fori_loop(1, parts, send, 0)
    arrived[slab] = block(sending, slab)[...]

    for copy in late:
        copy.wait()
    for b in range(0, bins, own):
        at = slice(b // own * lanes, (b // own + 1) * lanes)
        held = [background[pl.ds(b + g, rows, stride=bins), :] for g in range(own)]
        given[:, at] = jnp.concatenate(held, axis=0).T
        held = [counts[pl.ds(b + g, rows, stride=bins), :].astype(F32) for g in range(own)]
        counted[:, at] = jnp.concatenate(held, axis=0).T
    slices = own * parts
    for v in range(views):
        mix_rows[v * slices:(v + 1) * slices, :] = mix[v].T
    for v in range(views):
        for z in range(own):
            at = (v * own + z) * parts
            mix_t[at:at + parts, :] = mix_rows[pl.ds(v * slices + z, parts, stride=own), :]
    mixes_t = split(mix_t[...])
    mixes = split(mix_t[...].T)
    for v in range(views):
        turned = rx[v].T
        for c in range(2):
            for x in range(chips):
                rx_t[v, (c * chips + x) * own_rows:(c * chips + x + 1) * own_rows, :] = (
                    turned[(2 * x + c) * own_rows:(2 * x + c + 1) * own_rows]
                )
    tof_wide[...] = jnp.zeros_like(tof_wide)
    for z in range(own):
        for v in range(views):
            at = (z * views + v) * tof
            tof_wide[z * views + v, at:at + tof, :] = tof_ref[v]

    most = pltpu.make_async_remote_copy(
        src_ref=arrived.at[pl.ds(0, parts - 1)], dst_ref=arrived.at[pl.ds(0, parts - 1)],
        send_sem=send_sem, recv_sem=recv_sem, device_id={"slab": slab}, device_id_type=MESH,
    )
    most.wait_recv()

    group = lax.broadcasted_iota(jnp.int32, (parts, lanes), 1) // rows
    view_of = lax.broadcasted_iota(jnp.int32, (parts, lanes), 1) % rows // tof

    def swap(held):
        step = own // 2
        while step:
            swapped = list(held)
            low = group // step % 2 == 0
            for g in range(own):
                if g // step % 2 == 0:
                    a, b = held[g], held[g + step]
                    swapped[g] = jnp.where(low, a, pltpu.roll(b, step * rows, 1))
                    swapped[g + step] = jnp.where(low, pltpu.roll(a, lanes - step * rows, 1), b)
            held, step = swapped, step // 2
        return held

    staged[...] = arrived[...].astype(F32).reshape(staged.shape)
    for b in range(0, bins, own):
        at = slice(b // own * lanes, (b // own + 1) * lanes)
        held = swap([staged[pl.ds(b + g, parts, stride=bins), :] for g in range(own)])
        for v in range(views):
            for z in range(own):
                row = (v * own + z) * parts
                wide[row:row + parts, at] = jnp.where(view_of == v, held[z], 0.0).astype(BF16)
    total = dot(mixes[0], wide[...]) + dot(mixes[1], wide[...])
    high, low = split(counted[...] / (given[...] + total))
    spread = dot(mixes_t[0], high) + (dot(mixes_t[1], high) + dot(mixes_t[0], low))
    for b in range(0, bins, own):
        at = slice(b // own * lanes, (b // own + 1) * lanes)
        held = []
        for z in range(own):
            one = spread[z * parts:(z + 1) * parts, at]
            for v in range(1, views):
                row = (v * own + z) * parts
                one = jnp.where(view_of == v, spread[row:row + parts, at], one)
            held.append(one)
        held = swap(held)
        for g in range(own):
            staged[pl.ds(b + g, parts, stride=bins), :] = held[g]
    back[...] = staged[...].astype(BF16)

    def send_back(o, carry):
        peer = lax.rem(slab + o, parts)
        pltpu.make_async_remote_copy(
            src_ref=block(back, peer), dst_ref=block(back_in, slab), send_sem=back_send, recv_sem=back_recv,
            device_id={"slab": peer}, device_id_type=MESH,
        ).start()
        return carry

    lax.fori_loop(1, parts, send_back, 0)
    block(back_in, slab)[...] = block(back, slab)[...]
    few = pl.ds(0, (parts - 1) * bins)
    rest = pltpu.make_async_remote_copy(
        src_ref=back.at[few, :], dst_ref=back_in.at[few, :],
        send_sem=back_send, recv_sem=back_recv, device_id={"slab": slab}, device_id_type=MESH,
    )
    rest.wait_recv()

    def ours(which):
        return pl.ds(pl.multiple_of(which * half, half), half)

    def pair(z):
        return pltpu.make_async_remote_copy(
            src_ref=partial.at[z, ours(1 - core), :], dst_ref=other.at[z],
            send_sem=pair_send.at[z], recv_sem=pair_recv.at[z], device_id={"view": peers[0]}, device_id_type=MESH,
        )

    def leg(z, o):
        data = pltpu.make_async_remote_copy(
            src_ref=codes.at[z, o - 1], dst_ref=codes_in.at[z, o - 1],
            send_sem=code_send.at[z, o - 1], recv_sem=code_recv.at[z, o - 1],
            device_id={"view": peers[o]}, device_id_type=MESH,
        )
        scale = pltpu.make_async_remote_copy(
            src_ref=scales.at[z, o - 1], dst_ref=scales_in.at[z, o - 1],
            send_sem=scale_send.at[z, o - 1], recv_sem=scale_recv.at[z, o - 1],
            device_id={"view": peers[o]}, device_id_type=MESH,
        )
        return data, scale

    def rows_of(o):
        at = pl.multiple_of(lax.rem(chip + o, chips) * own_rows, own_rows)
        return pl.ds(at, own_rows), pl.ds(pl.multiple_of(core * half + at, own_rows), own_rows)

    def project(z):
        total = None
        for v in range(views):
            frames = dot(back_in[...], tof_wide[z * views + v]).astype(BF16)
            unrotated = dot(ry[v], frames).astype(BF16)
            term = dot(rx_t[v], unrotated, transposed=True)
            total = term if total is None else total + term
        partial[z] = total

    def onward(z):
        pair(z).wait_recv()
        for o in (2, 1, 3):
            theirs, ours_at = rows_of(o)
            held = partial[z, ours_at, :] + other[z, theirs, :]
            top = jnp.maximum(jnp.max(jnp.abs(held), axis=0, keepdims=True), 1e-30)
            codes[z, o - 1] = jnp.round(held * (LEVELS / top)).astype(jnp.int32).astype(jnp.int16)
            scales[z, o - 1] = top * (1.0 / LEVELS)
            for copy in leg(z, o):
                copy.start()

    for z in range(own):
        project(z)
        pair(z).start()
        if z > 0:
            onward(z - 1)
    onward(own - 1)
    for z in range(own):
        theirs, ours_at = rows_of(0)
        total = partial[z, ours_at, :] + other[z, theirs, :]
        for o in (1, 3, 2):
            for copy in leg(z, o):
                copy.wait_recv()
            total = total + codes_in[z, o - 1].astype(jnp.int32).astype(F32) * scales_in[z, o - 1]
        out_ref[z] = current[z] * total / sens[z]
    most.wait_send()
    rest.wait_send()
    for z in range(own):
        pair(z).wait_send()
        for o in range(1, chips):
            for copy in leg(z, o):
                copy.wait_send()


def local(image, sensitivity, resample_x, resample_y, tof_kernel, axial_mix, background, counts):
    parts = lax.axis_size("slab")
    own, own_rows, ny = sensitivity.shape
    views, tof, nx = tof_kernel.shape
    bins, planes = background.shape[2:]
    lanes = own * views * tof
    half = nx // 2
    others = half // own_rows - 1
    flat = views * tof * bins
    vm, dma, i32, i16 = pltpu.VMEM, pltpu.SemaphoreType.DMA, jnp.int32, jnp.int16
    hbm = pl.BlockSpec(memory_space=pltpu.HBM)
    return pl.pallas_call(
        kernel,
        out_shape=jax.ShapeDtypeStruct(sensitivity.shape, F32),
        in_specs=[hbm] * 8,
        out_specs=pl.BlockSpec(memory_space=pltpu.VMEM),
        scratch_shapes=[
            vm(image.shape, F32), vm(sensitivity.shape, F32),
            vm(resample_x.shape, BF16), vm(resample_y.shape, BF16), vm(tof_kernel.shape, BF16),
            vm(axial_mix.shape, F32), vm((flat, planes), F32), vm((flat, planes), i32),
            vm(sensitivity.shape, F32),
            vm((lanes, ny), F32), vm((ny, lanes), BF16), vm((parts, bins, lanes), BF16),
            vm((ny, lanes), BF16), vm((ny, lanes), BF16),
            vm((views * own * parts, bins // own * lanes), BF16),
            vm((planes, bins // own * lanes), F32), vm((planes, bins // own * lanes), F32),
            vm((ny, lanes), F32),
            vm((views * own * parts, planes), F32), vm((views * own * parts, planes), F32),
            vm((views, nx, nx), BF16), vm((own * views, lanes, nx), BF16),
            vm((own, nx, ny), F32), vm((own, half, ny), F32),
            vm((own, others, own_rows, ny), i16), vm((own, others, 1, ny), F32),
            vm((own, others, own_rows, ny), i16), vm((own, others, 1, ny), F32),
            dma((own + 8,)), dma, dma, dma, dma,
            dma((own,)), dma((own,)),
            dma((own, others)), dma((own, others)), dma((own, others)), dma((own, others)),
        ],
        compiler_params=pltpu.CompilerParams(collective_id=0, has_side_effects=True, vmem_limit_bytes=56 << 20),
        name="update",
    )(
        image, sensitivity, resample_x, resample_y, tof_kernel, axial_mix,
        background.reshape(flat, planes), counts.reshape(flat, planes),
    )


def solution(mesh):
    in_specs = (
        P("slab", None, None),
        P("slab", "view", None),
        P("view", None, None),
        P("view", None, None),
        P("view", None, None),
        P("view", None, None),
        P("view", None, "slab", None),
        P("view", None, "slab", None),
    )
    out_specs = P("slab", "view", None)
    return jax.shard_map(local, mesh=mesh, in_specs=in_specs, out_specs=out_specs, check_vma=False)
```

```python
import jax
import jax.numpy as jnp
from jax import lax
from jax.experimental import pallas as pl
from jax.experimental.pallas import tpu as pltpu
from jax.sharding import PartitionSpec as P

F32, BF16 = jnp.float32, jnp.bfloat16
MESH = pl.DeviceIdType.MESH
PAD = 16


def dot(a, b, transposed=False):
    dims = (((1,), (1 if transposed else 0,)), ((), ()))
    return lax.dot_general(a, b, dims, preferred_element_type=F32)


def split(a):
    high = a.astype(BF16)
    return high, (a - high.astype(F32)).astype(BF16)


def kernel(
    image_hbm, sens_hbm, rx_hbm, ry_hbm, tof_hbm, mix_hbm, background_hbm, counts_hbm, out_ref,
    image, sens, rx, ry, tof_ref, mix, background, counts, current,
    sums, sending, arrived, back, back_all, wide, given, counted, staged, mix_t, mix_rows,
    rx_near, tof_tall, tof_near, lines, partial, other,
    load_sem, send_sem, recv_sem, back_send, back_recv,
    pair_send, pair_recv, band_send, band_recv, share_send, share_recv,
):
    own, own_rows = sens.shape[0], sens.shape[1]
    views, tof = tof_ref.shape[0], tof_ref.shape[1]
    parts, bins, lanes = arrived.shape
    nx = rx.shape[2]
    chips = back_all.shape[0]
    width = nx // chips
    reach = rx_near.shape[2]
    rows = views * tof
    slab = lax.axis_index("slab")
    me = lax.axis_index("view")
    core, chip = me % 2, me // 2
    inner = slice(PAD, PAD + nx)

    loads = [
        pltpu.make_async_copy(image_hbm.at[0], image.at[0], load_sem.at[0]),
        pltpu.make_async_copy(ry_hbm, ry.at[0, :, inner, :], load_sem.at[1]),
        pltpu.make_async_copy(rx_hbm, rx.at[:, inner, :], load_sem.at[2]),
        pltpu.make_async_copy(tof_hbm, tof_ref, load_sem.at[3]),
    ]
    loads += [pltpu.make_async_copy(image_hbm.at[z], image.at[z], load_sem.at[3 + z]) for z in range(1, own)]
    late = [
        pltpu.make_async_copy(mix_hbm, mix, load_sem.at[own + 3]),
        pltpu.make_async_copy(background_hbm, background, load_sem.at[own + 4]),
        pltpu.make_async_copy(counts_hbm, counts, load_sem.at[own + 5]),
        pltpu.make_async_copy(sens_hbm, sens, load_sem.at[own + 6]),
        pltpu.make_async_copy(
            image_hbm.at[:, pl.ds(pl.multiple_of(me * own_rows, own_rows), own_rows), :], current, load_sem.at[own + 7]
        ),
    ]
    for copy in loads + late:
        copy.start()

    barrier = pltpu.get_barrier_semaphore()

    def greet(o, carry):
        peer = lax.rem(slab + o, parts)
        pl.semaphore_signal(barrier, inc=1, device_id={"slab": peer}, device_id_type=MESH)
        return carry

    lax.fori_loop(1, parts, greet, 0)
    peers = [me + 1 - 2 * core] + [lax.rem(chip + o, chips) * 2 + core for o in range(1, chips)]
    for edge in (slice(0, PAD), slice(PAD + nx, PAD + nx + PAD)):
        tof_tall[edge, :] = jnp.zeros((PAD, lanes), BF16)
        for v in range(views):
            rx[v, edge, :] = jnp.zeros((PAD, nx), BF16)
            ry[0, v, edge, :] = jnp.zeros((PAD, nx), BF16)
    for o in range(1, chips):
        ry[o] = jnp.zeros(ry.shape[1:], BF16)
    for peer in peers:
        pl.semaphore_signal(barrier, inc=1, device_id={"view": peer}, device_id_type=MESH)

    def near(which):
        at = pl.multiple_of(which * width, width)
        return pl.ds(at, reach), pl.ds(at, width)

    def bands(o):
        target = dict(device_id={"view": peers[o]}, device_id_type=MESH)
        there, across = near(peers[o] // 2)
        pieces = [
            (rx.at[:, there, across], rx_near.at[o]),
            (tof_tall.at[there, :], tof_near.at[o]),
        ]
        for b in range(chips):
            at = (slice(None), slice(b * width, b * width + reach), slice(b * width, (b + 1) * width))
            pieces.append((ry.at[(0,) + at], ry.at[(o,) + at]))
        return [
            pltpu.make_async_remote_copy(
                src_ref=a, dst_ref=b, send_sem=band_send.at[o - 1, n], recv_sem=band_recv.at[o - 1, n], **target
            )
            for n, (a, b) in enumerate(pieces)
        ]

    here, along = near(chip)
    mine_near = [
        pltpu.make_async_copy(rx.at[:, here, along], rx_near.at[0], load_sem.at[0]),
        pltpu.make_async_copy(tof_tall.at[here, :], tof_near.at[0], load_sem.at[1]),
    ]
    for z in range(own):
        if z == 0:
            for copy in loads[:4]:
                copy.wait()
            tall = jnp.concatenate([tof_ref[...].astype(F32).reshape(rows, nx)] * own, axis=0)
            tof_tall[inner, :] = tall.T.astype(BF16)
            for copy in mine_near:
                copy.start()
        else:
            loads[3 + z].wait()
        low = image[z].astype(BF16)
        for v in range(views):
            along_y = dot(low, ry[0, v, inner, :]).astype(BF16)
            rotated = dot(rx[v, inner, :], along_y).astype(BF16)
            at = (z * views + v) * tof
            sums[at:at + tof, :] = dot(tof_ref[v], rotated)
        if z == own // 2 - 1:
            pl.semaphore_wait(barrier, parts - 1 + len(peers))
            for o in (1, 3, 2):
                for copy in bands(o):
                    copy.start()
    sending[...] = sums[...].T.astype(BF16)

    def block(ref, i):
        return ref.at[pl.ds(pl.multiple_of(i * bins, bins), bins), :]

    def send(o, carry):
        peer = lax.rem(slab + o, parts)
        pltpu.make_async_remote_copy(
            src_ref=block(sending, peer), dst_ref=arrived.at[slab], send_sem=send_sem, recv_sem=recv_sem,
            device_id={"slab": peer}, device_id_type=MESH,
        ).start()
        return carry

    lax.fori_loop(1, parts, send, 0)
    arrived[slab] = block(sending, slab)[...]

    for copy in late:
        copy.wait()
    for b in range(0, bins, own):
        at = slice(b // own * lanes, (b // own + 1) * lanes)
        held = [background[pl.ds(b + g, rows, stride=bins), :] for g in range(own)]
        given[:, at] = jnp.concatenate(held, axis=0).T
        held = [counts[pl.ds(b + g, rows, stride=bins), :].astype(F32) for g in range(own)]
        counted[:, at] = jnp.concatenate(held, axis=0).T
    slices = own * parts
    for v in range(views):
        mix_rows[v * slices:(v + 1) * slices, :] = mix[v].T
    for v in range(views):
        for z in range(own):
            at = (v * own + z) * parts
            mix_t[at:at + parts, :] = mix_rows[pl.ds(v * slices + z, parts, stride=own), :]
    mixes_t = split(mix_t[...])
    mixes = split(mix_t[...].T)
    for copy in mine_near:
        copy.wait()

    most = pltpu.make_async_remote_copy(
        src_ref=arrived.at[pl.ds(0, parts - 1)], dst_ref=arrived.at[pl.ds(0, parts - 1)],
        send_sem=send_sem, recv_sem=recv_sem, device_id={"slab": slab}, device_id_type=MESH,
    )
    most.wait_recv()

    group = lax.broadcasted_iota(jnp.int32, (parts, lanes), 1) // rows
    view_of = lax.broadcasted_iota(jnp.int32, (parts, lanes), 1) % rows // tof

    def swap(held):
        step = own // 2
        while step:
            swapped = list(held)
            low = group // step % 2 == 0
            for g in range(own):
                if g // step % 2 == 0:
                    a, b = held[g], held[g + step]
                    swapped[g] = jnp.where(low, a, pltpu.roll(b, step * rows, 1))
                    swapped[g + step] = jnp.where(low, pltpu.roll(a, lanes - step * rows, 1), b)
            held, step = swapped, step // 2
        return held

    staged[...] = arrived[...].astype(F32).reshape(staged.shape)
    for b in range(0, bins, own):
        at = slice(b // own * lanes, (b // own + 1) * lanes)
        held = swap([staged[pl.ds(b + g, parts, stride=bins), :] for g in range(own)])
        for v in range(views):
            for z in range(own):
                row = (v * own + z) * parts
                wide[row:row + parts, at] = jnp.where(view_of == v, held[z], 0.0).astype(BF16)
    total = dot(mixes[0], wide[...]) + dot(mixes[1], wide[...])
    high, low = split(counted[...] / (given[...] + total))
    spread = dot(mixes_t[0], high) + (dot(mixes_t[1], high) + dot(mixes_t[0], low))
    for b in range(0, bins, own):
        at = slice(b // own * lanes, (b // own + 1) * lanes)
        held = []
        for z in range(own):
            one = spread[z * parts:(z + 1) * parts, at]
            for v in range(1, views):
                row = (v * own + z) * parts
                one = jnp.where(view_of == v, spread[row:row + parts, at], one)
            held.append(one)
        held = swap(held)
        for g in range(own):
            staged[pl.ds(b + g, parts, stride=bins), :] = held[g]
    back[...] = staged[...].astype(BF16)

    def send_back(o, carry):
        peer = lax.rem(slab + o, parts)
        pltpu.make_async_remote_copy(
            src_ref=block(back, peer), dst_ref=block(back_all.at[0], slab), send_sem=back_send, recv_sem=back_recv,
            device_id={"slab": peer}, device_id_type=MESH,
        ).start()
        return carry

    lax.fori_loop(1, parts, send_back, 0)
    block(back_all.at[0], slab)[...] = block(back, slab)[...]
    few = pl.ds(0, (parts - 1) * bins)
    rest = pltpu.make_async_remote_copy(
        src_ref=back.at[few, :], dst_ref=back_all.at[0, few, :],
        send_sem=back_send, recv_sem=back_recv, device_id={"slab": slab}, device_id_type=MESH,
    )
    rest.wait_recv()

    def share(o):
        return pltpu.make_async_remote_copy(
            src_ref=back_all.at[0], dst_ref=back_all.at[o], send_sem=share_send.at[o - 1], recv_sem=share_recv.at[o - 1],
            device_id={"view": peers[o]}, device_id_type=MESH,
        )

    for o in (1, 3, 2):
        share(o).start()
    part = lax.broadcasted_iota(jnp.int32, (reach, lanes), 1) // tof
    for o in (0, 1, 3, 2):
        if o:
            for copy in bands(o):
                copy.wait_recv()
            share(o).wait_recv()
        weights = tof_near[o].astype(F32)
        for v in range(views):
            chosen = [jnp.where(part == z * views + v, weights, 0.0).astype(BF16) for z in range(own)]
            frames = dot(jnp.concatenate(chosen, axis=0), back_all[o], transposed=True).astype(BF16)
            unrotated = dot(frames, ry[o, v, inner, :], transposed=True).astype(BF16)
            at = (o * views + v) * reach
            for z in range(own):
                lines[z, at:at + reach, :] = unrotated[z * reach:(z + 1) * reach]

    def half(which):
        return pl.ds(pl.multiple_of(which * own_rows, own_rows), own_rows)

    def pair(z):
        return pltpu.make_async_remote_copy(
            src_ref=partial.at[z, half(1 - core), :], dst_ref=other.at[z],
            send_sem=pair_send.at[z], recv_sem=pair_recv.at[z], device_id={"view": peers[0]}, device_id_type=MESH,
        )

    turned = rx_near[...].reshape(chips * views * reach, width).T
    for z in range(own):
        partial[z] = dot(turned, lines[z])
        pair(z).start()
    for z in range(own):
        pair(z).wait_recv()
        out_ref[z] = current[z] * (partial[z, half(core), :] + other[z]) / sens[z]
    most.wait_send()
    rest.wait_send()
    for z in range(own):
        pair(z).wait_send()
    for o in range(1, chips):
        share(o).wait_send()
        for copy in bands(o):
            copy.wait_send()


def local(image, sensitivity, resample_x, resample_y, tof_kernel, axial_mix, background, counts):
    parts = lax.axis_size("slab")
    own, own_rows, ny = sensitivity.shape
    views, tof, nx = tof_kernel.shape
    bins, planes = background.shape[2:]
    lanes = own * views * tof
    chips = lax.axis_size("view") // 2
    width = nx // chips
    reach = width + 2 * PAD
    flat = views * tof * bins
    vm, dma, i32 = pltpu.VMEM, pltpu.SemaphoreType.DMA, jnp.int32
    hbm = pl.BlockSpec(memory_space=pltpu.HBM)
    return pl.pallas_call(
        kernel,
        out_shape=jax.ShapeDtypeStruct(sensitivity.shape, F32),
        in_specs=[hbm] * 8,
        out_specs=pl.BlockSpec(memory_space=pltpu.VMEM),
        scratch_shapes=[
            vm(image.shape, F32), vm(sensitivity.shape, F32),
            vm((views, nx + 2 * PAD, nx), BF16), vm((chips, views, nx + 2 * PAD, nx), BF16), vm(tof_kernel.shape, BF16),
            vm(axial_mix.shape, F32), vm((flat, planes), F32), vm((flat, planes), i32),
            vm(sensitivity.shape, F32),
            vm((lanes, ny), F32), vm((ny, lanes), BF16), vm((parts, bins, lanes), BF16),
            vm((ny, lanes), BF16), vm((chips, ny, lanes), BF16),
            vm((views * own * parts, bins // own * lanes), BF16),
            vm((planes, bins // own * lanes), F32), vm((planes, bins // own * lanes), F32),
            vm((ny, lanes), F32),
            vm((views * own * parts, planes), F32), vm((views * own * parts, planes), F32),
            vm((chips, views, reach, width), BF16), vm((nx + 2 * PAD, lanes), BF16), vm((chips, reach, lanes), BF16),
            vm((own, chips * views * reach, ny), BF16), vm((own, width, ny), F32), vm((own, own_rows, ny), F32),
            dma((own + 8,)), dma, dma, dma, dma,
            dma((own,)), dma((own,)),
            dma((chips - 1, chips + 2)), dma((chips - 1, chips + 2)), dma((chips - 1,)), dma((chips - 1,)),
        ],
        compiler_params=pltpu.CompilerParams(collective_id=0, has_side_effects=True, vmem_limit_bytes=56 << 20),
        name="update",
    )(
        image, sensitivity, resample_x, resample_y, tof_kernel, axial_mix,
        background.reshape(flat, planes), counts.reshape(flat, planes),
    )


def solution(mesh):
    in_specs = (
        P("slab", None, None),
        P("slab", "view", None),
        P("view", None, None),
        P("view", None, None),
        P("view", None, None),
        P("view", None, None),
        P("view", None, "slab", None),
        P("view", None, "slab", None),
    )
    out_specs = P("slab", "view", None)
    return jax.shard_map(local, mesh=mesh, in_specs=in_specs, out_specs=out_specs, check_vma=False)
```

```python
import jax
import jax.numpy as jnp
from jax import lax
from jax.experimental import pallas as pl
from jax.experimental.pallas import tpu as pltpu
from jax.sharding import PartitionSpec as P

F32, BF16 = jnp.float32, jnp.bfloat16
MESH = pl.DeviceIdType.MESH
PAD = 16
PIECE = 2 * PAD
RING = 8


def dot(a, b, transposed=False):
    dims = (((1,), (1 if transposed else 0,)), ((), ()))
    return lax.dot_general(a, b, dims, preferred_element_type=F32)


def split(a):
    high = a.astype(BF16)
    return high, (a - high.astype(F32)).astype(BF16)


def kernel(
    image_hbm, sens_hbm, rx_hbm, ry_hbm, tof_hbm, mix_hbm, background_hbm, counts_hbm, out_ref,
    image, sens, rx, ry, tof_ref, mix, background, counts, current,
    sums, sending, arrived, back, back_all, wide, given, counted, staged, mix_t, mix_rows,
    rx_near, tof_tall, tof_near, rx_pack, ry_pack, rx_in, ry_in, lines, partial, other,
    load_sem, send_sem, recv_sem, back_send, back_recv,
    pair_send, pair_recv, band_send, band_recv, share_send, share_recv,
):
    own, own_rows = sens.shape[0], sens.shape[1]
    views, tof = tof_ref.shape[0], tof_ref.shape[1]
    parts, bins, lanes = arrived.shape
    nx = rx.shape[2]
    chips = back_all.shape[0]
    width = nx // chips
    reach = rx_near.shape[2]
    rows = views * tof
    slab = lax.axis_index("slab")
    me = lax.axis_index("view")
    core, chip = me % 2, me // 2
    inner = slice(PAD, PAD + nx)

    loads = [
        pltpu.make_async_copy(image_hbm.at[0], image.at[0], load_sem.at[0]),
        pltpu.make_async_copy(ry_hbm, ry.at[0, :, inner, :], load_sem.at[1]),
        pltpu.make_async_copy(rx_hbm, rx.at[:, inner, :], load_sem.at[2]),
        pltpu.make_async_copy(tof_hbm, tof_ref, load_sem.at[3]),
    ]
    loads += [pltpu.make_async_copy(image_hbm.at[z], image.at[z], load_sem.at[3 + z]) for z in range(1, own)]
    late = [
        pltpu.make_async_copy(mix_hbm, mix, load_sem.at[own + 3]),
        pltpu.make_async_copy(background_hbm, background, load_sem.at[own + 4]),
        pltpu.make_async_copy(counts_hbm, counts, load_sem.at[own + 5]),
        pltpu.make_async_copy(sens_hbm, sens, load_sem.at[own + 6]),
        pltpu.make_async_copy(
            image_hbm.at[:, pl.ds(pl.multiple_of(me * own_rows, own_rows), own_rows), :], current, load_sem.at[own + 7]
        ),
    ]
    for copy in loads + late:
        copy.start()

    barrier = pltpu.get_barrier_semaphore()

    def greet(o, carry):
        peer = lax.rem(slab + o, parts)
        pl.semaphore_signal(barrier, inc=1, device_id={"slab": peer}, device_id_type=MESH)
        return carry

    lax.fori_loop(1, parts, greet, 0)
    peers = [me + 1 - 2 * core] + [lax.rem(chip + o, chips) * 2 + core for o in range(1, chips)]
    for edge in (slice(0, PAD), slice(PAD + nx, PAD + nx + PAD)):
        tof_tall[edge, :] = jnp.zeros((PAD, lanes), BF16)
        for v in range(views):
            rx[v, edge, :] = jnp.zeros((PAD, nx), BF16)
            ry[0, v, edge, :] = jnp.zeros((PAD, nx), BF16)
    for peer in peers:
        pl.semaphore_signal(barrier, inc=1, device_id={"view": peer}, device_id_type=MESH)

    def near(which):
        at = pl.multiple_of(which * width, width)
        return pl.ds(at, reach), pl.ds(at, width)

    def bands(o):
        target = dict(device_id={"view": peers[o]}, device_id_type=MESH)
        to = peers[o] // 2
        pieces = [
            (rx_pack.at[to], rx_in.at[o - 1]),
            (tof_tall.at[near(to)[0], :], tof_near.at[o]),
            (ry_pack, ry_in.at[o - 1]),
        ]
        return [
            pltpu.make_async_remote_copy(
                src_ref=a, dst_ref=b, send_sem=band_send.at[o - 1, n], recv_sem=band_recv.at[o - 1, n], **target
            )
            for n, (a, b) in enumerate(pieces)
        ]

    part = lax.broadcasted_iota(jnp.int32, (PIECE, width), 1) // PIECE
    keep = [jnp.where(part == g, 1.0, 0.0).astype(BF16) for g in range(width // PIECE)]

    def pack(ref, b):
        cols = slice(b * width, (b + 1) * width)
        halves = []
        for h in range(2):
            rows_at = [b * width + (g + h) * PIECE for g in range(len(keep))]
            halves.append(sum(ref[r:r + PIECE, cols] * m for r, m in zip(rows_at, keep)))
        return jnp.concatenate(halves, axis=0)

    def unpack(held):
        first, second = held[:PIECE], held[PIECE:]
        rows_of = [first * keep[0]]
        for g in range(1, len(keep)):
            rows_of.append(first * keep[g] + second * keep[g - 1])
        rows_of.append(second * keep[-1])
        return jnp.concatenate(rows_of, axis=0)

    here, along = near(chip)
    mine_near = [
        pltpu.make_async_copy(rx.at[:, here, along], rx_near.at[0], load_sem.at[0]),
        pltpu.make_async_copy(tof_tall.at[here, :], tof_near.at[0], load_sem.at[1]),
    ]
    for z in range(own):
        if z == 0:
            for copy in loads[:4]:
                copy.wait()
            tall = jnp.concatenate([tof_ref[...].astype(F32).reshape(rows, nx)] * own, axis=0)
            tof_tall[inner, :] = tall.T.astype(BF16)
            for copy in mine_near:
                copy.start()
            for b in range(chips):
                for v in range(views):
                    rx_pack[b, v] = pack(rx.at[v], b)
                    ry_pack[b, v] = pack(ry.at[0, v], b)
        else:
            loads[3 + z].wait()
        low = image[z].astype(BF16)
        for v in range(views):
            along_y = dot(low, ry[0, v, inner, :]).astype(BF16)
            rotated = dot(rx[v, inner, :], along_y).astype(BF16)
            at = (z * views + v) * tof
            sums[at:at + tof, :] = dot(tof_ref[v], rotated)
        if z == own // 2 - 1:
            pl.semaphore_wait(barrier, parts - 1 + len(peers))
            for o in (1, 3, 2):
                for copy in bands(o):
                    copy.start()
    sending[...] = sums[...].T.astype(BF16)

    def block(ref, i):
        return ref.at[pl.ds(pl.multiple_of(i * bins, bins), bins), :]

    rings = parts // RING
    far = [(dy, dz) for dy in range(rings) for dz in range(RING) if dy or dz]
    far.sort(key=lambda d: -min(d[0], rings - d[0]) - min(d[1], RING - d[1]))

    def peer_at(dy, dz):
        return lax.rem(slab // RING + dy, rings) * RING + lax.rem(slab + dz, RING)

    for dy, dz in far:
        peer = peer_at(dy, dz)
        pltpu.make_async_remote_copy(
            src_ref=block(sending, peer), dst_ref=arrived.at[slab], send_sem=send_sem, recv_sem=recv_sem,
            device_id={"slab": peer}, device_id_type=MESH,
        ).start()
    arrived[slab] = block(sending, slab)[...]

    for copy in late:
        copy.wait()
    for b in range(0, bins, own):
        at = slice(b // own * lanes, (b // own + 1) * lanes)
        held = [background[pl.ds(b + g, rows, stride=bins), :] for g in range(own)]
        given[:, at] = jnp.concatenate(held, axis=0).T
        held = [counts[pl.ds(b + g, rows, stride=bins), :].astype(F32) for g in range(own)]
        counted[:, at] = jnp.concatenate(held, axis=0).T
    slices = own * parts
    for v in range(views):
        mix_rows[v * slices:(v + 1) * slices, :] = mix[v].T
    for v in range(views):
        for z in range(own):
            at = (v * own + z) * parts
            mix_t[at:at + parts, :] = mix_rows[pl.ds(v * slices + z, parts, stride=own), :]
    mixes_t = split(mix_t[...])
    mixes = split(mix_t[...].T)
    for copy in mine_near:
        copy.wait()
    for o in range(1, chips):
        for v in range(views):
            ry[o, v] = jnp.zeros(ry.shape[2:], BF16)

    most = pltpu.make_async_remote_copy(
        src_ref=arrived.at[pl.ds(0, parts - 1)], dst_ref=arrived.at[pl.ds(0, parts - 1)],
        send_sem=send_sem, recv_sem=recv_sem, device_id={"slab": slab}, device_id_type=MESH,
    )
    most.wait_recv()

    group = lax.broadcasted_iota(jnp.int32, (parts, lanes), 1) // rows
    view_of = lax.broadcasted_iota(jnp.int32, (parts, lanes), 1) % rows // tof

    def swap(held):
        step = own // 2
        while step:
            swapped = list(held)
            low = group // step % 2 == 0
            for g in range(own):
                if g // step % 2 == 0:
                    a, b = held[g], held[g + step]
                    swapped[g] = jnp.where(low, a, pltpu.roll(b, step * rows, 1))
                    swapped[g + step] = jnp.where(low, pltpu.roll(a, lanes - step * rows, 1), b)
            held, step = swapped, step // 2
        return held

    staged[...] = arrived[...].astype(F32).reshape(staged.shape)
    for b in range(0, bins, own):
        at = slice(b // own * lanes, (b // own + 1) * lanes)
        held = swap([staged[pl.ds(b + g, parts, stride=bins), :] for g in range(own)])
        for v in range(views):
            for z in range(own):
                row = (v * own + z) * parts
                wide[row:row + parts, at] = jnp.where(view_of == v, held[z], 0.0).astype(BF16)
    total = dot(mixes[0], wide[...]) + dot(mixes[1], wide[...])
    high, low = split(counted[...] / (given[...] + total))
    spread = dot(mixes_t[0], high) + (dot(mixes_t[1], high) + dot(mixes_t[0], low))
    for b in range(0, bins, own):
        at = slice(b // own * lanes, (b // own + 1) * lanes)
        held = []
        for z in range(own):
            one = spread[z * parts:(z + 1) * parts, at]
            for v in range(1, views):
                row = (v * own + z) * parts
                one = jnp.where(view_of == v, spread[row:row + parts, at], one)
            held.append(one)
        held = swap(held)
        for g in range(own):
            staged[pl.ds(b + g, parts, stride=bins), :] = held[g]
    back[...] = staged[...].astype(BF16)

    for dy, dz in far:
        peer = peer_at(dy, dz)
        pltpu.make_async_remote_copy(
            src_ref=block(back, peer), dst_ref=block(back_all.at[0], slab), send_sem=back_send, recv_sem=back_recv,
            device_id={"slab": peer}, device_id_type=MESH,
        ).start()
    block(back_all.at[0], slab)[...] = block(back, slab)[...]
    for o in (1, 3, 2):
        for copy in bands(o):
            copy.wait_recv()
        for v in range(views):
            rx_near[o, v] = unpack(rx_in[o - 1, v])
            for b in range(chips):
                ry[o, v, b * width:b * width + reach, b * width:(b + 1) * width] = unpack(ry_in[o - 1, b, v])
    turned = rx_near[...].reshape(chips * views * reach, width).T
    few = pl.ds(0, (parts - 1) * bins)
    rest = pltpu.make_async_remote_copy(
        src_ref=back.at[few, :], dst_ref=back_all.at[0, few, :],
        send_sem=back_send, recv_sem=back_recv, device_id={"slab": slab}, device_id_type=MESH,
    )
    rest.wait_recv()

    def share(o):
        return pltpu.make_async_remote_copy(
            src_ref=back_all.at[0], dst_ref=back_all.at[o], send_sem=share_send.at[o - 1], recv_sem=share_recv.at[o - 1],
            device_id={"view": peers[o]}, device_id_type=MESH,
        )

    for o in (1, 3, 2):
        share(o).start()
    which = lax.broadcasted_iota(jnp.int32, (reach, lanes), 1) // tof
    for o in (0, 1, 3, 2):
        if o:
            share(o).wait_recv()
        weights = tof_near[o].astype(F32)
        for v in range(views):
            chosen = [jnp.where(which == z * views + v, weights, 0.0).astype(BF16) for z in range(own)]
            frames = dot(jnp.concatenate(chosen, axis=0), back_all[o], transposed=True).astype(BF16)
            unrotated = dot(frames, ry[o, v, inner, :], transposed=True).astype(BF16)
            at = (o * views + v) * reach
            for z in range(own):
                lines[z, at:at + reach, :] = unrotated[z * reach:(z + 1) * reach]

    def half(at):
        return pl.ds(pl.multiple_of(at * own_rows, own_rows), own_rows)

    def pair(z):
        return pltpu.make_async_remote_copy(
            src_ref=partial.at[z, half(1 - core), :], dst_ref=other.at[z],
            send_sem=pair_send.at[z], recv_sem=pair_recv.at[z], device_id={"view": peers[0]}, device_id_type=MESH,
        )

    for z in range(own):
        partial[z] = dot(turned, lines[z])
        pair(z).start()
    for z in range(own):
        pair(z).wait_recv()
        out_ref[z] = current[z] * (partial[z, half(core), :] + other[z]) / sens[z]
    most.wait_send()
    rest.wait_send()
    for z in range(own):
        pair(z).wait_send()
    for o in range(1, chips):
        share(o).wait_send()
        for copy in bands(o):
            copy.wait_send()


def local(image, sensitivity, resample_x, resample_y, tof_kernel, axial_mix, background, counts):
    parts = lax.axis_size("slab")
    own, own_rows, ny = sensitivity.shape
    views, tof, nx = tof_kernel.shape
    bins, planes = background.shape[2:]
    lanes = own * views * tof
    chips = lax.axis_size("view") // 2
    width = nx // chips
    reach = width + 2 * PAD
    flat = views * tof * bins
    vm, dma, i32 = pltpu.VMEM, pltpu.SemaphoreType.DMA, jnp.int32
    hbm = pl.BlockSpec(memory_space=pltpu.HBM)
    return pl.pallas_call(
        kernel,
        out_shape=jax.ShapeDtypeStruct(sensitivity.shape, F32),
        in_specs=[hbm] * 8,
        out_specs=pl.BlockSpec(memory_space=pltpu.VMEM),
        scratch_shapes=[
            vm(image.shape, F32), vm(sensitivity.shape, F32),
            vm((views, nx + 2 * PAD, nx), BF16), vm((chips, views, nx + 2 * PAD, nx), BF16), vm(tof_kernel.shape, BF16),
            vm(axial_mix.shape, F32), vm((flat, planes), F32), vm((flat, planes), i32),
            vm(sensitivity.shape, F32),
            vm((lanes, ny), F32), vm((ny, lanes), BF16), vm((parts, bins, lanes), BF16),
            vm((ny, lanes), BF16), vm((chips, ny, lanes), BF16),
            vm((views * own * parts, bins // own * lanes), BF16),
            vm((planes, bins // own * lanes), F32), vm((planes, bins // own * lanes), F32),
            vm((ny, lanes), F32),
            vm((views * own * parts, planes), F32), vm((views * own * parts, planes), F32),
            vm((chips, views, reach, width), BF16), vm((nx + 2 * PAD, lanes), BF16), vm((chips, reach, lanes), BF16),
            vm((chips, views, 2 * PIECE, width), BF16), vm((chips, views, 2 * PIECE, width), BF16),
            vm((chips - 1, views, 2 * PIECE, width), BF16), vm((chips - 1, chips, views, 2 * PIECE, width), BF16),
            vm((own, chips * views * reach, ny), BF16), vm((own, width, ny), F32), vm((own, own_rows, ny), F32),
            dma((own + 8,)), dma, dma, dma, dma,
            dma((own,)), dma((own,)),
            dma((chips - 1, 3)), dma((chips - 1, 3)), dma((chips - 1,)), dma((chips - 1,)),
        ],
        compiler_params=pltpu.CompilerParams(collective_id=0, has_side_effects=True, vmem_limit_bytes=56 << 20),
        name="update",
    )(
        image, sensitivity, resample_x, resample_y, tof_kernel, axial_mix,
        background.reshape(flat, planes), counts.reshape(flat, planes),
    )


def solution(mesh):
    in_specs = (
        P("slab", None, None),
        P("slab", "view", None),
        P("view", None, None),
        P("view", None, None),
        P("view", None, None),
        P("view", None, None),
        P("view", None, "slab", None),
        P("view", None, "slab", None),
    )
    out_specs = P("slab", "view", None)
    return jax.shard_map(local, mesh=mesh, in_specs=in_specs, out_specs=out_specs, check_vma=False)
```

```python
import jax
import jax.numpy as jnp
from jax import lax
from jax.experimental import pallas as pl
from jax.experimental.pallas import tpu as pltpu
from jax.sharding import PartitionSpec as P

F32, BF16 = jnp.float32, jnp.bfloat16
MESH = pl.DeviceIdType.MESH
PAD = 16
PIECE = 2 * PAD
RING = 8


def dot(a, b, transposed=False):
    dims = (((1,), (1 if transposed else 0,)), ((), ()))
    return lax.dot_general(a, b, dims, preferred_element_type=F32)


def split(a):
    high = a.astype(BF16)
    return high, (a - high.astype(F32)).astype(BF16)


def kernel(
    image_hbm, sens_hbm, rx_hbm, ry_hbm, tof_hbm, mix_hbm, background_hbm, counts_hbm, out_ref,
    image, sens, rx, ry, tof_ref, mix, background, counts, current,
    sums, sending, arrived, back, back_all, wide, given, counted, staged, mix_t, mix_rows,
    rx_near, tof_tall, tof_near, rx_pack, ry_pack, rx_in, ry_in, lines, partial, other,
    load_sem, send_sem, recv_sem, back_send, back_recv,
    pair_send, pair_recv, band_send, band_recv, share_send, share_recv,
):
    own, own_rows = sens.shape[0], sens.shape[1]
    views, tof = tof_ref.shape[0], tof_ref.shape[1]
    parts, bins, lanes = arrived.shape
    nx = rx.shape[2]
    chips = back_all.shape[0]
    width = nx // chips
    reach = rx_near.shape[2]
    rows = views * tof
    slab = lax.axis_index("slab")
    me = lax.axis_index("view")
    core, chip = me % 2, me // 2
    inner = slice(PAD, PAD + nx)

    loads = [
        pltpu.make_async_copy(image_hbm.at[0], image.at[0], load_sem.at[0]),
        pltpu.make_async_copy(ry_hbm, ry.at[0, :, inner, :], load_sem.at[1]),
        pltpu.make_async_copy(rx_hbm, rx.at[:, inner, :], load_sem.at[2]),
        pltpu.make_async_copy(tof_hbm, tof_ref, load_sem.at[3]),
    ]
    loads += [pltpu.make_async_copy(image_hbm.at[z], image.at[z], load_sem.at[3 + z]) for z in range(1, own)]
    late = [
        pltpu.make_async_copy(mix_hbm, mix, load_sem.at[own + 3]),
        pltpu.make_async_copy(background_hbm, background, load_sem.at[own + 4]),
        pltpu.make_async_copy(counts_hbm, counts, load_sem.at[own + 5]),
        pltpu.make_async_copy(sens_hbm, sens, load_sem.at[own + 6]),
        pltpu.make_async_copy(
            image_hbm.at[:, pl.ds(pl.multiple_of(me * own_rows, own_rows), own_rows), :], current, load_sem.at[own + 7]
        ),
    ]
    for copy in loads + late:
        copy.start()

    barrier = pltpu.get_barrier_semaphore()

    def greet(o, carry):
        peer = lax.rem(slab + o, parts)
        pl.semaphore_signal(barrier, inc=1, device_id={"slab": peer}, device_id_type=MESH)
        return carry

    lax.fori_loop(1, parts, greet, 0)
    peers = [me + 1 - 2 * core] + [lax.rem(chip + o, chips) * 2 + core for o in range(1, chips)]
    for edge in (slice(0, PAD), slice(PAD + nx, PAD + nx + PAD)):
        tof_tall[edge, :] = jnp.zeros((PAD, lanes), BF16)
        for v in range(views):
            rx[v, edge, :] = jnp.zeros((PAD, nx), BF16)
            ry[0, v, edge, :] = jnp.zeros((PAD, nx), BF16)
    for peer in peers:
        pl.semaphore_signal(barrier, inc=1, device_id={"view": peer}, device_id_type=MESH)

    def near(which):
        at = pl.multiple_of(which * width, width)
        return pl.ds(at, reach), pl.ds(at, width)

    def bands(o):
        target = dict(device_id={"view": peers[o]}, device_id_type=MESH)
        to = peers[o] // 2
        pieces = [
            (rx_pack.at[to], rx_in.at[o - 1]),
            (tof_tall.at[near(to)[0], :], tof_near.at[o]),
            (ry_pack, ry_in.at[o - 1]),
        ]
        return [
            pltpu.make_async_remote_copy(
                src_ref=a, dst_ref=b, send_sem=band_send.at[o - 1, n], recv_sem=band_recv.at[o - 1, n], **target
            )
            for n, (a, b) in enumerate(pieces)
        ]

    part = lax.broadcasted_iota(jnp.int32, (PIECE, width), 1) // PIECE
    keep = [jnp.where(part == g, 1.0, 0.0).astype(BF16) for g in range(width // PIECE)]

    def pack(ref, b):
        cols = slice(b * width, (b + 1) * width)
        halves = []
        for h in range(2):
            rows_at = [b * width + (g + h) * PIECE for g in range(len(keep))]
            halves.append(sum(ref[r:r + PIECE, cols] * m for r, m in zip(rows_at, keep)))
        return jnp.concatenate(halves, axis=0)

    def unpack(held):
        first, second = held[:PIECE], held[PIECE:]
        rows_of = [first * keep[0]]
        for g in range(1, len(keep)):
            rows_of.append(first * keep[g] + second * keep[g - 1])
        rows_of.append(second * keep[-1])
        return jnp.concatenate(rows_of, axis=0)

    here, along = near(chip)
    mine_near = [
        pltpu.make_async_copy(rx.at[:, here, along], rx_near.at[0], load_sem.at[0]),
        pltpu.make_async_copy(tof_tall.at[here, :], tof_near.at[0], load_sem.at[1]),
    ]
    for z in range(own):
        if z == 0:
            for copy in loads[:4]:
                copy.wait()
            tall = jnp.concatenate([tof_ref[...].astype(F32).reshape(rows, nx)] * own, axis=0)
            tof_tall[inner, :] = tall.T.astype(BF16)
            for copy in mine_near:
                copy.start()
            for b in range(chips):
                for v in range(views):
                    rx_pack[b, v] = pack(rx.at[v], b)
                    ry_pack[b, v] = pack(ry.at[0, v], b)
        else:
            loads[3 + z].wait()
        low = image[z].astype(BF16)
        for v in range(views):
            along_y = dot(low, ry[0, v, inner, :]).astype(BF16)
            rotated = dot(rx[v, inner, :], along_y).astype(BF16)
            at = (z * views + v) * tof
            sums[at:at + tof, :] = dot(tof_ref[v], rotated)
        if z == own // 2 - 1:
            pl.semaphore_wait(barrier, parts - 1 + len(peers))
            for o in (1, 3, 2):
                for copy in bands(o):
                    copy.start()
    sending[...] = sums[...].T.astype(BF16)

    def block(ref, i):
        return ref.at[pl.ds(pl.multiple_of(i * bins, bins), bins), :]

    rings = parts // RING
    far = [(dy, dz) for dy in range(rings) for dz in range(RING) if dy or dz]
    far.sort(key=lambda d: -min(d[0], rings - d[0]) - min(d[1], RING - d[1]))

    def peer_at(dy, dz):
        return lax.rem(slab // RING + dy, rings) * RING + lax.rem(slab + dz, RING)

    for dy, dz in far:
        peer = peer_at(dy, dz)
        pltpu.make_async_remote_copy(
            src_ref=block(sending, peer), dst_ref=arrived.at[slab], send_sem=send_sem, recv_sem=recv_sem,
            device_id={"slab": peer}, device_id_type=MESH,
        ).start()
    arrived[slab] = block(sending, slab)[...]

    for copy in late:
        copy.wait()
    for b in range(0, bins, own):
        at = slice(b // own * lanes, (b // own + 1) * lanes)
        held = [background[pl.ds(b + g, rows, stride=bins), :] for g in range(own)]
        given[:, at] = jnp.concatenate(held, axis=0).T
        held = [counts[pl.ds(b + g, rows, stride=bins), :].astype(F32) for g in range(own)]
        counted[:, at] = jnp.concatenate(held, axis=0).T
    slices = own * parts
    for v in range(views):
        mix_rows[v * slices:(v + 1) * slices, :] = mix[v].T
    for v in range(views):
        for z in range(own):
            at = (v * own + z) * parts
            mix_t[at:at + parts, :] = mix_rows[pl.ds(v * slices + z, parts, stride=own), :]
    mixes_t = split(mix_t[...])
    mixes = split(mix_t[...].T)
    for copy in mine_near:
        copy.wait()
    for o in range(1, chips):
        for v in range(views):
            ry[o, v] = jnp.zeros(ry.shape[2:], BF16)

    most = pltpu.make_async_remote_copy(
        src_ref=arrived.at[pl.ds(0, parts - 1)], dst_ref=arrived.at[pl.ds(0, parts - 1)],
        send_sem=send_sem, recv_sem=recv_sem, device_id={"slab": slab}, device_id_type=MESH,
    )
    most.wait_recv()

    group = lax.broadcasted_iota(jnp.int32, (parts, lanes), 1) // rows
    view_of = lax.broadcasted_iota(jnp.int32, (parts, lanes), 1) % rows // tof

    def swap(held):
        step = own // 2
        while step:
            swapped = list(held)
            low = group // step % 2 == 0
            for g in range(own):
                if g // step % 2 == 0:
                    a, b = held[g], held[g + step]
                    swapped[g] = jnp.where(low, a, pltpu.roll(b, step * rows, 1))
                    swapped[g + step] = jnp.where(low, pltpu.roll(a, lanes - step * rows, 1), b)
            held, step = swapped, step // 2
        return held

    staged[...] = arrived[...].astype(F32).reshape(staged.shape)
    for b in range(0, bins, own):
        at = slice(b // own * lanes, (b // own + 1) * lanes)
        held = swap([staged[pl.ds(b + g, parts, stride=bins), :] for g in range(own)])
        for v in range(views):
            for z in range(own):
                row = (v * own + z) * parts
                wide[row:row + parts, at] = jnp.where(view_of == v, held[z], 0.0).astype(BF16)
    total = dot(mixes[0], wide[...]) + dot(mixes[1], wide[...])
    high, low = split(counted[...] / (given[...] + total))
    spread = dot(mixes_t[0], high) + (dot(mixes_t[1], high) + dot(mixes_t[0], low))
    for b in range(0, bins, own):
        at = slice(b // own * lanes, (b // own + 1) * lanes)
        held = []
        for z in range(own):
            one = spread[z * parts:(z + 1) * parts, at]
            for v in range(1, views):
                row = (v * own + z) * parts
                one = jnp.where(view_of == v, spread[row:row + parts, at], one)
            held.append(one)
        held = swap(held)
        for g in range(own):
            staged[pl.ds(b + g, parts, stride=bins), :] = held[g]
    back[...] = staged[...].astype(BF16)

    for dy, dz in far:
        peer = peer_at(dy, dz)
        pltpu.make_async_remote_copy(
            src_ref=block(back, peer), dst_ref=block(back_all.at[0], slab), send_sem=back_send, recv_sem=back_recv,
            device_id={"slab": peer}, device_id_type=MESH,
        ).start()
    block(back_all.at[0], slab)[...] = block(back, slab)[...]
    for o in (1, 3, 2):
        for copy in bands(o):
            copy.wait_recv()
        for v in range(views):
            rx_near[o, v] = unpack(rx_in[o - 1, v])
            for b in range(chips):
                ry[o, v, b * width:b * width + reach, b * width:(b + 1) * width] = unpack(ry_in[o - 1, b, v])
    turned = rx_near[...].reshape(chips * views * reach, width).T
    few = pl.ds(0, (parts - 1) * bins)
    rest = pltpu.make_async_remote_copy(
        src_ref=back.at[few, :], dst_ref=back_all.at[0, few, :],
        send_sem=back_send, recv_sem=back_recv, device_id={"slab": slab}, device_id_type=MESH,
    )
    rest.wait_recv()

    def share(o):
        return pltpu.make_async_remote_copy(
            src_ref=back_all.at[0], dst_ref=back_all.at[o], send_sem=share_send.at[o - 1], recv_sem=share_recv.at[o - 1],
            device_id={"view": peers[o]}, device_id_type=MESH,
        )

    for o in (1, 3, 2):
        share(o).start()
    which = lax.broadcasted_iota(jnp.int32, (reach, lanes), 1) // tof
    for o in (0, 1, 3, 2):
        if o:
            share(o).wait_recv()
        weights = tof_near[o].astype(F32)
        for v in range(views):
            chosen = [jnp.where(which == z * views + v, weights, 0.0).astype(BF16) for z in range(own)]
            frames = dot(jnp.concatenate(chosen, axis=0), back_all[o], transposed=True).astype(BF16)
            unrotated = dot(frames, ry[o, v, inner, :], transposed=True).astype(BF16)
            at = (o * views + v) * reach
            for z in range(own):
                lines[z, at:at + reach, :] = unrotated[z * reach:(z + 1) * reach]

    def half(at):
        return pl.ds(pl.multiple_of(at * own_rows, own_rows), own_rows)

    def pair(z):
        return pltpu.make_async_remote_copy(
            src_ref=partial.at[z, half(1 - core), :], dst_ref=other.at[z],
            send_sem=pair_send.at[z], recv_sem=pair_recv.at[z], device_id={"view": peers[0]}, device_id_type=MESH,
        )

    for z in range(own):
        partial[z] = dot(turned, lines[z])
        pair(z).start()
    for z in range(own):
        pair(z).wait_recv()
        out_ref[z] = current[z] * (partial[z, half(core), :] + other[z]) / sens[z]
    most.wait_send()
    rest.wait_send()
    for z in range(own):
        pair(z).wait_send()
    for o in range(1, chips):
        share(o).wait_send()
        for copy in bands(o):
            copy.wait_send()


def local(image, sensitivity, resample_x, resample_y, tof_kernel, axial_mix, background, counts):
    parts = lax.axis_size("slab")
    own, own_rows, ny = sensitivity.shape
    views, tof, nx = tof_kernel.shape
    bins, planes = background.shape[2:]
    lanes = own * views * tof
    chips = lax.axis_size("view") // 2
    width = nx // chips
    reach = width + 2 * PAD
    flat = views * tof * bins
    vm, dma, i32 = pltpu.VMEM, pltpu.SemaphoreType.DMA, jnp.int32
    hbm = pl.BlockSpec(memory_space=pltpu.HBM)
    return pl.pallas_call(
        kernel,
        out_shape=jax.ShapeDtypeStruct(sensitivity.shape, F32),
        in_specs=[hbm] * 8,
        out_specs=pl.BlockSpec(memory_space=pltpu.VMEM),
        scratch_shapes=[
            vm(image.shape, F32), vm(sensitivity.shape, F32),
            vm((views, nx + 2 * PAD, nx), BF16), vm((chips, views, nx + 2 * PAD, nx), BF16), vm(tof_kernel.shape, BF16),
            vm(axial_mix.shape, F32), vm((flat, planes), F32), vm((flat, planes), i32),
            vm(sensitivity.shape, F32),
            vm((lanes, ny), F32), vm((ny, lanes), BF16), vm((parts, bins, lanes), BF16),
            vm((ny, lanes), BF16), vm((chips, ny, lanes), BF16),
            vm((views * own * parts, bins // own * lanes), BF16),
            vm((planes, bins // own * lanes), F32), vm((planes, bins // own * lanes), F32),
            vm((ny, lanes), F32),
            vm((views * own * parts, planes), F32), vm((views * own * parts, planes), F32),
            vm((chips, views, reach, width), BF16), vm((nx + 2 * PAD, lanes), BF16), vm((chips, reach, lanes), BF16),
            vm((chips, views, 2 * PIECE, width), BF16), vm((chips, views, 2 * PIECE, width), BF16),
            vm((chips - 1, views, 2 * PIECE, width), BF16), vm((chips - 1, chips, views, 2 * PIECE, width), BF16),
            vm((own, chips * views * reach, ny), BF16), vm((own, width, ny), F32), vm((own, own_rows, ny), F32),
            dma((own + 8,)), dma, dma, dma, dma,
            dma((own,)), dma((own,)),
            dma((chips - 1, 3)), dma((chips - 1, 3)), dma((chips - 1,)), dma((chips - 1,)),
        ],
        compiler_params=pltpu.CompilerParams(collective_id=0, has_side_effects=True, vmem_limit_bytes=48 << 20),
        name="update",
    )(*[
        pltpu.with_memory_space_constraint(a, pltpu.HBM)
        for a in (
            image, sensitivity, resample_x, resample_y, tof_kernel, axial_mix,
            background.reshape(flat, planes), counts.reshape(flat, planes),
        )
    ])


def solution(mesh):
    in_specs = (
        P("slab", None, None),
        P("slab", "view", None),
        P("view", None, None),
        P("view", None, None),
        P("view", None, None),
        P("view", None, None),
        P("view", None, "slab", None),
        P("view", None, "slab", None),
    )
    out_specs = P("slab", "view", None)
    return jax.shard_map(local, mesh=mesh, in_specs=in_specs, out_specs=out_specs, check_vma=False)
```

```python
import jax
import jax.numpy as jnp
from jax import lax
from jax.experimental import pallas as pl
from jax.experimental.pallas import tpu as pltpu
from jax.sharding import PartitionSpec as P

F32, BF16 = jnp.float32, jnp.bfloat16
MESH = pl.DeviceIdType.MESH
PAD = 16
PIECE = 2 * PAD
RING = 8


def dot(a, b, transposed=False):
    dims = (((1,), (1 if transposed else 0,)), ((), ()))
    return lax.dot_general(a, b, dims, preferred_element_type=F32)


def split(a):
    high = a.astype(BF16)
    return high, (a - high.astype(F32)).astype(BF16)


def kernel(
    image_hbm, sens_hbm, rx_hbm, ry_hbm, tof_hbm, mix_hbm, background_hbm, counts_hbm, out_ref,
    image, sens, rx, ry, tof_ref, mix, background, counts, current,
    sums, sending, arrived, back, back_all, wide, given, counted, staged, mix_t, mix_rows,
    rx_near, tof_tall, tof_near, rx_pack, ry_pack, rx_in, ry_in, lines, partial, other,
    load_sem, send_sem, recv_sem, back_send, back_recv,
    pair_send, pair_recv, band_send, band_recv, share_send, share_recv,
):
    own, own_rows = sens.shape[0], sens.shape[1]
    views, tof = tof_ref.shape[0], tof_ref.shape[1]
    parts, rank, lanes = arrived.shape[1:]
    bins = 2 * rank
    nx = rx.shape[2]
    chips = back_all.shape[0]
    width = nx // chips
    reach = rx_near.shape[2]
    slab = lax.axis_index("slab")
    me = lax.axis_index("view")
    core, chip = me % 2, me // 2
    inner = slice(PAD, PAD + nx)

    loads = [
        pltpu.make_async_copy(image_hbm.at[0], image.at[0], load_sem.at[0]),
        pltpu.make_async_copy(ry_hbm, ry.at[0, :, inner, :], load_sem.at[1]),
        pltpu.make_async_copy(rx_hbm, rx.at[:, inner, :], load_sem.at[2]),
        pltpu.make_async_copy(tof_hbm, tof_ref, load_sem.at[3]),
    ]
    loads += [pltpu.make_async_copy(image_hbm.at[z], image.at[z], load_sem.at[3 + z]) for z in range(1, own)]
    late = [
        pltpu.make_async_copy(mix_hbm, mix, load_sem.at[own + 3]),
        pltpu.make_async_copy(background_hbm, background, load_sem.at[own + 4]),
        pltpu.make_async_copy(counts_hbm, counts, load_sem.at[own + 5]),
        pltpu.make_async_copy(sens_hbm, sens, load_sem.at[own + 6]),
        pltpu.make_async_copy(
            image_hbm.at[:, pl.ds(pl.multiple_of(me * own_rows, own_rows), own_rows), :], current, load_sem.at[own + 7]
        ),
    ]
    for copy in loads + late:
        copy.start()

    barrier = pltpu.get_barrier_semaphore()

    def greet(o, carry):
        peer = lax.rem(slab + o, parts)
        pl.semaphore_signal(barrier, inc=1, device_id={"slab": peer}, device_id_type=MESH)
        return carry

    lax.fori_loop(1, parts, greet, 0)
    peers = [me + 1 - 2 * core] + [lax.rem(chip + o, chips) * 2 + core for o in range(1, chips)]
    for edge in (slice(0, PAD), slice(PAD + nx, PAD + nx + PAD)):
        tof_tall[edge, :] = jnp.zeros((PAD, lanes), BF16)
        for v in range(views):
            rx[v, edge, :] = jnp.zeros((PAD, nx), BF16)
            ry[0, v, edge, :] = jnp.zeros((PAD, nx), BF16)
    for peer in peers:
        pl.semaphore_signal(barrier, inc=1, device_id={"view": peer}, device_id_type=MESH)

    def near(which):
        at = pl.multiple_of(which * width, width)
        return pl.ds(at, reach), pl.ds(at, width)

    def bands(o):
        target = dict(device_id={"view": peers[o]}, device_id_type=MESH)
        to = peers[o] // 2
        pieces = [
            (rx_pack.at[to], rx_in.at[o - 1]),
            (tof_tall.at[near(to)[0], :], tof_near.at[o]),
            (ry_pack, ry_in.at[o - 1]),
        ]
        return [
            pltpu.make_async_remote_copy(
                src_ref=a, dst_ref=b, send_sem=band_send.at[o - 1, n], recv_sem=band_recv.at[o - 1, n], **target
            )
            for n, (a, b) in enumerate(pieces)
        ]

    part = lax.broadcasted_iota(jnp.int32, (PIECE, width), 1) // PIECE
    keep = [jnp.where(part == g, 1.0, 0.0).astype(BF16) for g in range(width // PIECE)]

    def pack(ref, b):
        cols = slice(b * width, (b + 1) * width)
        halves = []
        for h in range(2):
            rows_at = [b * width + (g + h) * PIECE for g in range(len(keep))]
            halves.append(sum(ref[r:r + PIECE, cols] * m for r, m in zip(rows_at, keep)))
        return jnp.concatenate(halves, axis=0)

    def unpack(held):
        first, second = held[:PIECE], held[PIECE:]
        rows_of = [first * keep[0]]
        for g in range(1, len(keep)):
            rows_of.append(first * keep[g] + second * keep[g - 1])
        rows_of.append(second * keep[-1])
        return jnp.concatenate(rows_of, axis=0)

    here, along = near(chip)
    mine_near = [
        pltpu.make_async_copy(rx.at[:, here, along], rx_near.at[0], load_sem.at[0]),
        pltpu.make_async_copy(tof_tall.at[here, :], tof_near.at[0], load_sem.at[1]),
    ]
    rings = parts // RING
    far = [(dy, dz) for dy in range(rings) for dz in range(RING) if dy or dz]
    far.sort(key=lambda d: -min(d[0], rings - d[0]) - min(d[1], RING - d[1]))

    def peer_at(dy, dz):
        return lax.rem(slab // RING + dy, rings) * RING + lax.rem(slab + dz, RING)

    def block(ref, i):
        return ref.at[i]

    def send(v):
        for dy, dz in far:
            peer = peer_at(dy, dz)
            pltpu.make_async_remote_copy(
                src_ref=block(sending.at[v], peer), dst_ref=arrived.at[v, slab],
                send_sem=send_sem.at[v], recv_sem=recv_sem.at[v],
                device_id={"slab": peer}, device_id_type=MESH,
            ).start()
        arrived[v, slab] = block(sending.at[v], slab)[...]

    def sent(v):
        most = arrived.at[v, pl.ds(0, parts - 1)]
        return pltpu.make_async_remote_copy(
            src_ref=most, dst_ref=most, send_sem=send_sem.at[v], recv_sem=recv_sem.at[v],
            device_id={"slab": slab}, device_id_type=MESH,
        )

    def send_back(v):
        for dy, dz in far:
            peer = peer_at(dy, dz)
            pltpu.make_async_remote_copy(
                src_ref=block(back.at[v], peer), dst_ref=block(back_all.at[0, v], slab),
                send_sem=back_send.at[v], recv_sem=back_recv.at[v],
                device_id={"slab": peer}, device_id_type=MESH,
            ).start()
        block(back_all.at[0, v], slab)[...] = block(back.at[v], slab)[...]

    def sent_back(v):
        few = pl.ds(0, parts - 1)
        return pltpu.make_async_remote_copy(
            src_ref=back.at[v, few], dst_ref=back_all.at[0, v, few],
            send_sem=back_send.at[v], recv_sem=back_recv.at[v],
            device_id={"slab": slab}, device_id_type=MESH,
        )

    side = lax.broadcasted_iota(jnp.int32, (parts, rank, lanes), 2) < lanes // 2
    for v in range(views):
        for z in range(own):
            if v == 0 and z == 0:
                for copy in loads[:4]:
                    copy.wait()
                tall = [tof_ref[u].astype(F32) for u in range(views) for n in range(own)]
                tof_tall[inner, :] = jnp.concatenate(tall, axis=0).T.astype(BF16)
                for copy in mine_near:
                    copy.start()
                for b in range(chips):
                    for u in range(views):
                        rx_pack[b, u] = pack(rx.at[u], b)
                        ry_pack[b, u] = pack(ry.at[0, u], b)
            elif v == 0:
                loads[3 + z].wait()
            low = image[z].astype(BF16)
            along_y = dot(low, ry[0, v, inner, :]).astype(BF16)
            rotated = dot(rx[v, inner, :], along_y).astype(BF16)
            held = dot(tof_ref[v], rotated)
            for h in range(2):
                at = (h * own + z) * tof
                sums[at:at + tof, :] = held
        held = sums[...].T.reshape(parts, bins, lanes)
        held = jnp.where(side, held[:, :rank], held[:, rank:])
        sending[v] = held.astype(BF16)
        if v == 0:
            pl.semaphore_wait(barrier, parts - 1 + len(peers))
        send(v)
        if v == 0:
            for o in (1, 3, 2):
                for copy in bands(o):
                    copy.start()

    for copy in late:
        copy.wait()
    runs = rank // own
    for v in range(views):
        for n in range(runs):
            at = slice(n * lanes, (n + 1) * lanes)
            first = [v * tof * bins + h * rank + n * own + g for h in range(2) for g in range(own)]
            held = [background[pl.ds(b, tof, stride=bins), :] for b in first]
            given[v, :, at] = jnp.concatenate(held, axis=0).T
            held = [counts[pl.ds(b, tof, stride=bins), :].astype(F32) for b in first]
            counted[v, :, at] = jnp.concatenate(held, axis=0).T
    slices = own * parts
    for v in range(views):
        mix_rows[v * slices:(v + 1) * slices, :] = mix[v].T
    for v in range(views):
        for z in range(own):
            at = (v * own + z) * parts
            mix_t[at:at + parts, :] = mix_rows[pl.ds(v * slices + z, parts, stride=own), :]
    mixes_t = [split(mix_t[v * slices:(v + 1) * slices, :]) for v in range(views)]
    mixes = [split(mix_t[v * slices:(v + 1) * slices, :].T) for v in range(views)]
    for copy in mine_near:
        copy.wait()
    group = lax.broadcasted_iota(jnp.int32, (parts, lanes), 1) // tof

    def swap(held):
        step = own // 2
        while step:
            swapped = list(held)
            low = group // step % 2 == 0
            for g in range(own):
                if g // step % 2 == 0:
                    a, b = held[g], held[g + step]
                    swapped[g] = jnp.where(low, a, pltpu.roll(b, step * tof, 1))
                    swapped[g + step] = jnp.where(low, pltpu.roll(a, lanes - step * tof, 1), b)
            held, step = swapped, step // 2
        return held

    for v in range(views):
        sent(v).wait_recv()
        staged[...] = arrived[v].astype(F32).reshape(staged.shape)
        for n in range(runs):
            at = slice(n * lanes, (n + 1) * lanes)
            held = swap([staged[pl.ds(n * own + g, parts, stride=rank), :] for g in range(own)])
            for z in range(own):
                wide[z * parts:(z + 1) * parts, at] = held[z].astype(BF16)
        total = dot(mixes[v][0], wide[...]) + dot(mixes[v][1], wide[...])
        high, low = split(counted[v] / (given[v] + total))
        spread = dot(mixes_t[v][0], high) + (dot(mixes_t[v][1], high) + dot(mixes_t[v][0], low))
        for n in range(runs):
            at = slice(n * lanes, (n + 1) * lanes)
            held = swap([spread[z * parts:(z + 1) * parts, at] for z in range(own)])
            for g in range(own):
                staged[pl.ds(n * own + g, parts, stride=rank), :] = held[g]
        back[v] = staged[...].reshape(parts, rank, lanes).astype(BF16)
        send_back(v)
    for o in range(1, chips):
        for v in range(views):
            ry[o, v] = jnp.zeros(ry.shape[2:], BF16)
    for o in (1, 3, 2):
        for copy in bands(o):
            copy.wait_recv()
        for v in range(views):
            rx_near[o, v] = unpack(rx_in[o - 1, v])
            for b in range(chips):
                ry[o, v, b * width:b * width + reach, b * width:(b + 1) * width] = unpack(ry_in[o - 1, b, v])
    turned = rx_near[...].reshape(chips * views * reach, width).T
    def share(o, v):
        return pltpu.make_async_remote_copy(
            src_ref=back_all.at[0, v], dst_ref=back_all.at[o, v],
            send_sem=share_send.at[o - 1, v], recv_sem=share_recv.at[o - 1, v],
            device_id={"view": peers[o]}, device_id_type=MESH,
        )

    which = lax.broadcasted_iota(jnp.int32, (reach, lanes), 1) // tof

    def project(o, v):
        if o:
            share(o, v).wait_recv()
        held = back_all[o, v].astype(F32).reshape(parts * rank, lanes)
        turn = pltpu.roll(held, lanes // 2, 1)
        pair_of = [held, turn] if v == 0 else [turn, held]
        pair_of = [h.reshape(parts, rank, lanes) for h in pair_of]
        spread_out = jnp.concatenate(pair_of, axis=1).reshape(parts * bins, lanes).astype(BF16)
        weights = tof_near[o].astype(F32)
        chosen = [jnp.where(which == v * own + z, weights, 0.0).astype(BF16) for z in range(own)]
        frames = dot(jnp.concatenate(chosen, axis=0), spread_out, transposed=True).astype(BF16)
        unrotated = dot(frames, ry[o, v, inner, :], transposed=True).astype(BF16)
        at = (o * views + v) * reach
        for z in range(own):
            lines[z, at:at + reach, :] = unrotated[z * reach:(z + 1) * reach]

    for v in range(views):
        sent_back(v).wait_recv()
        for o in (1, 3, 2):
            share(o, v).start()
        project(0, v)
    for v in range(views):
        for o in (1, 3, 2):
            project(o, v)

    def half(at):
        return pl.ds(pl.multiple_of(at * own_rows, own_rows), own_rows)

    def pair(z):
        return pltpu.make_async_remote_copy(
            src_ref=partial.at[z, half(1 - core), :], dst_ref=other.at[z],
            send_sem=pair_send.at[z], recv_sem=pair_recv.at[z], device_id={"view": peers[0]}, device_id_type=MESH,
        )

    for z in range(own):
        partial[z] = dot(turned, lines[z])
        pair(z).start()
    for z in range(own):
        pair(z).wait_recv()
        out_ref[z] = current[z] * (partial[z, half(core), :] + other[z]) / sens[z]
    for v in range(views):
        sent(v).wait_send()
        sent_back(v).wait_send()
    for z in range(own):
        pair(z).wait_send()
    for o in range(1, chips):
        for v in range(views):
            share(o, v).wait_send()
        for copy in bands(o):
            copy.wait_send()


def local(image, sensitivity, resample_x, resample_y, tof_kernel, axial_mix, background, counts):
    parts = lax.axis_size("slab")
    own, own_rows, ny = sensitivity.shape
    views, tof, nx = tof_kernel.shape
    bins, planes = background.shape[2:]
    lanes = own * views * tof
    chips = lax.axis_size("view") // 2
    width = nx // chips
    reach = width + 2 * PAD
    flat = views * tof * bins
    packed = ny // 2
    columns = bins * tof
    vm, dma, i32 = pltpu.VMEM, pltpu.SemaphoreType.DMA, jnp.int32
    hbm = pl.BlockSpec(memory_space=pltpu.HBM)
    return pl.pallas_call(
        kernel,
        out_shape=jax.ShapeDtypeStruct(sensitivity.shape, F32),
        in_specs=[hbm] * 8,
        out_specs=pl.BlockSpec(memory_space=pltpu.VMEM),
        scratch_shapes=[
            vm(image.shape, F32), vm(sensitivity.shape, F32),
            vm((views, nx + 2 * PAD, nx), BF16), vm((chips, views, nx + 2 * PAD, nx), BF16), vm(tof_kernel.shape, BF16),
            vm(axial_mix.shape, F32), vm((flat, planes), F32), vm((flat, planes), i32),
            vm(sensitivity.shape, F32),
            vm((lanes, ny), F32), vm((views, parts, bins // 2, lanes), BF16), vm((views, parts, bins // 2, lanes), BF16),
            vm((views, parts, bins // 2, lanes), BF16), vm((chips, views, parts, bins // 2, lanes), BF16),
            vm((own * parts, columns), BF16),
            vm((views, planes, columns), F32), vm((views, planes, columns), F32),
            vm((packed, lanes), F32),
            vm((views * own * parts, planes), F32), vm((views * own * parts, planes), F32),
            vm((chips, views, reach, width), BF16), vm((nx + 2 * PAD, lanes), BF16), vm((chips, reach, lanes), BF16),
            vm((chips, views, 2 * PIECE, width), BF16), vm((chips, views, 2 * PIECE, width), BF16),
            vm((chips - 1, views, 2 * PIECE, width), BF16), vm((chips - 1, chips, views, 2 * PIECE, width), BF16),
            vm((own, chips * views * reach, ny), BF16), vm((own, width, ny), F32), vm((own, own_rows, ny), F32),
            dma((own + 8,)), dma((views,)), dma((views,)), dma((views,)), dma((views,)),
            dma((own,)), dma((own,)),
            dma((chips - 1, 3)), dma((chips - 1, 3)), dma((chips - 1, views)), dma((chips - 1, views)),
        ],
        compiler_params=pltpu.CompilerParams(collective_id=0, has_side_effects=True, vmem_limit_bytes=48 << 20),
        name="update",
    )(*[
        pltpu.with_memory_space_constraint(a, pltpu.HBM)
        for a in (
            image, sensitivity, resample_x, resample_y, tof_kernel, axial_mix,
            background.reshape(flat, planes), counts.reshape(flat, planes),
        )
    ])


def solution(mesh):
    in_specs = (
        P("slab", None, None),
        P("slab", "view", None),
        P("view", None, None),
        P("view", None, None),
        P("view", None, None),
        P("view", None, None),
        P("view", None, "slab", None),
        P("view", None, "slab", None),
    )
    out_specs = P("slab", "view", None)
    return jax.shard_map(local, mesh=mesh, in_specs=in_specs, out_specs=out_specs, check_vma=False)
```

```python
import jax
import jax.numpy as jnp
from jax import lax
from jax.experimental import pallas as pl
from jax.experimental.pallas import tpu as pltpu
from jax.sharding import PartitionSpec as P

F32, BF16 = jnp.float32, jnp.bfloat16
MESH = pl.DeviceIdType.MESH
PAD = 16
PIECE = 2 * PAD
RING = 8


def dot(a, b, transposed=False):
    dims = (((1,), (1 if transposed else 0,)), ((), ()))
    return lax.dot_general(a, b, dims, preferred_element_type=F32)


def split(a):
    high = a.astype(BF16)
    return high, (a - high.astype(F32)).astype(BF16)


def kernel(
    image_hbm, sens_hbm, rx_hbm, ry_hbm, tof_hbm, mix_hbm, background_hbm, counts_hbm, out_ref,
    image, sens, rx, ry, tof_ref, mix, background, counts, current,
    sums, sending, arrived, back, back_all, wide, given, counted, staged, mix_t, mix_rows,
    rx_near, tof_tall, tof_near, rx_pack, ry_pack, rx_in, ry_in, lines, partial, other,
    load_sem, send_sem, recv_sem, back_send, back_recv,
    pair_send, pair_recv, band_send, band_recv, share_send, share_recv,
):
    own, own_rows = sens.shape[0], sens.shape[1]
    views, tof = tof_ref.shape[0], tof_ref.shape[1]
    parts, rank, lanes = arrived.shape[1:]
    bins = 2 * rank
    nx = rx.shape[2]
    chips = back_all.shape[0]
    width = nx // chips
    reach = rx_near.shape[2]
    slab = lax.axis_index("slab")
    me = lax.axis_index("view")
    core, chip = me % 2, me // 2
    inner = slice(PAD, PAD + nx)

    loads = [
        pltpu.make_async_copy(image_hbm.at[0], image.at[0], load_sem.at[0]),
        pltpu.make_async_copy(ry_hbm, ry.at[0, :, inner, :], load_sem.at[1]),
        pltpu.make_async_copy(rx_hbm, rx.at[:, inner, :], load_sem.at[2]),
        pltpu.make_async_copy(tof_hbm, tof_ref, load_sem.at[3]),
    ]
    loads += [pltpu.make_async_copy(image_hbm.at[z], image.at[z], load_sem.at[3 + z]) for z in range(1, own)]
    late = [
        pltpu.make_async_copy(mix_hbm, mix, load_sem.at[own + 3]),
        pltpu.make_async_copy(background_hbm, background, load_sem.at[own + 4]),
        pltpu.make_async_copy(counts_hbm, counts, load_sem.at[own + 5]),
        pltpu.make_async_copy(sens_hbm, sens, load_sem.at[own + 6]),
        pltpu.make_async_copy(
            image_hbm.at[:, pl.ds(pl.multiple_of(me * own_rows, own_rows), own_rows), :], current, load_sem.at[own + 7]
        ),
    ]
    for copy in loads + late:
        copy.start()

    barrier = pltpu.get_barrier_semaphore()

    def greet(o, carry):
        peer = lax.rem(slab + o, parts)
        pl.semaphore_signal(barrier, inc=1, device_id={"slab": peer}, device_id_type=MESH)
        return carry

    lax.fori_loop(1, parts, greet, 0)
    peers = [me + 1 - 2 * core] + [lax.rem(chip + o, chips) * 2 + core for o in range(1, chips)]
    for edge in (slice(0, PAD), slice(PAD + nx, PAD + nx + PAD)):
        tof_tall[edge, :] = jnp.zeros((PAD, lanes), BF16)
        for v in range(views):
            rx[v, edge, :] = jnp.zeros((PAD, nx), BF16)
            ry[0, v, edge, :] = jnp.zeros((PAD, nx), BF16)
    for peer in peers:
        pl.semaphore_signal(barrier, inc=1, device_id={"view": peer}, device_id_type=MESH)

    def near(which):
        at = pl.multiple_of(which * width, width)
        return pl.ds(at, reach), pl.ds(at, width)

    def bands(o):
        target = dict(device_id={"view": peers[o]}, device_id_type=MESH)
        to = peers[o] // 2
        pieces = [
            (rx_pack.at[to], rx_in.at[o - 1]),
            (tof_tall.at[near(to)[0], :], tof_near.at[o]),
            (ry_pack, ry_in.at[o - 1]),
        ]
        return [
            pltpu.make_async_remote_copy(
                src_ref=a, dst_ref=b, send_sem=band_send.at[o - 1, n], recv_sem=band_recv.at[o - 1, n], **target
            )
            for n, (a, b) in enumerate(pieces)
        ]

    for o in range(1, chips):
        for v in range(views):
            ry[o, v] = jnp.zeros(ry.shape[2:], BF16)
    part = lax.broadcasted_iota(jnp.int32, (PIECE, width), 1) // PIECE
    keep = [jnp.where(part == g, 1.0, 0.0).astype(BF16) for g in range(width // PIECE)]

    def pack(ref, b):
        cols = slice(b * width, (b + 1) * width)
        halves = []
        for h in range(2):
            rows_at = [b * width + (g + h) * PIECE for g in range(len(keep))]
            halves.append(sum(ref[r:r + PIECE, cols] * m for r, m in zip(rows_at, keep)))
        return jnp.concatenate(halves, axis=0)

    def unpack(held):
        first, second = held[:PIECE], held[PIECE:]
        rows_of = [first * keep[0]]
        for g in range(1, len(keep)):
            rows_of.append(first * keep[g] + second * keep[g - 1])
        rows_of.append(second * keep[-1])
        return jnp.concatenate(rows_of, axis=0)

    here, along = near(chip)
    mine_near = [
        pltpu.make_async_copy(rx.at[:, here, along], rx_near.at[0], load_sem.at[0]),
        pltpu.make_async_copy(tof_tall.at[here, :], tof_near.at[0], load_sem.at[1]),
    ]
    rings = parts // RING
    far = [(dy, dz) for dy in range(rings) for dz in range(RING) if dy or dz]
    far.sort(key=lambda d: -min(d[0], rings - d[0]) - min(d[1], RING - d[1]))

    def peer_at(dy, dz):
        return lax.rem(slab // RING + dy, rings) * RING + lax.rem(slab + dz, RING)

    def block(ref, i):
        return ref.at[i]

    def send(v):
        for dy, dz in far:
            peer = peer_at(dy, dz)
            pltpu.make_async_remote_copy(
                src_ref=block(sending.at[v], peer), dst_ref=arrived.at[v, slab],
                send_sem=send_sem.at[v], recv_sem=recv_sem.at[v],
                device_id={"slab": peer}, device_id_type=MESH,
            ).start()
        arrived[v, slab] = block(sending.at[v], slab)[...]

    def sent(v):
        most = arrived.at[v, pl.ds(0, parts - 1)]
        return pltpu.make_async_remote_copy(
            src_ref=most, dst_ref=most, send_sem=send_sem.at[v], recv_sem=recv_sem.at[v],
            device_id={"slab": slab}, device_id_type=MESH,
        )

    def send_back(v):
        for dy, dz in far:
            peer = peer_at(dy, dz)
            pltpu.make_async_remote_copy(
                src_ref=block(back.at[v], peer), dst_ref=block(back_all.at[0, v], slab),
                send_sem=back_send.at[v], recv_sem=back_recv.at[v],
                device_id={"slab": peer}, device_id_type=MESH,
            ).start()
        block(back_all.at[0, v], slab)[...] = block(back.at[v], slab)[...]

    def sent_back(v):
        few = pl.ds(0, parts - 1)
        return pltpu.make_async_remote_copy(
            src_ref=back.at[v, few], dst_ref=back_all.at[0, v, few],
            send_sem=back_send.at[v], recv_sem=back_recv.at[v],
            device_id={"slab": slab}, device_id_type=MESH,
        )

    side = lax.broadcasted_iota(jnp.int32, (parts, rank, lanes), 2) < lanes // 2
    for v in range(views):
        for z in range(own):
            if v == 0 and z == 0:
                for copy in loads[:4]:
                    copy.wait()
            elif v == 0:
                loads[3 + z].wait()
            low = image[z].astype(BF16)
            along_y = dot(low, ry[0, v, inner, :]).astype(BF16)
            rotated = dot(rx[v, inner, :], along_y).astype(BF16)
            held = dot(tof_ref[v], rotated)
            for h in range(2):
                at = (h * own + z) * tof
                sums[at:at + tof, :] = held
        held = sums[...].T.reshape(parts, bins, lanes)
        held = jnp.where(side, held[:, :rank], held[:, rank:])
        sending[v] = held.astype(BF16)
        if v == 0:
            pl.semaphore_wait(barrier, parts - 1 + len(peers))
        send(v)
        if v == 0:
            tall = [tof_ref[u].astype(F32) for u in range(views) for n in range(own)]
            tof_tall[inner, :] = jnp.concatenate(tall, axis=0).T.astype(BF16)
            for copy in mine_near:
                copy.start()
            for b in range(chips):
                for u in range(views):
                    rx_pack[b, u] = pack(rx.at[u], b)
                    ry_pack[b, u] = pack(ry.at[0, u], b)
            for o in (1, 3, 2):
                for copy in bands(o):
                    copy.start()

    for copy in late:
        copy.wait()
    runs = rank // own
    for v in range(views):
        for n in range(runs):
            at = slice(n * lanes, (n + 1) * lanes)
            first = [v * tof * bins + h * rank + n * own + g for h in range(2) for g in range(own)]
            held = [background[pl.ds(b, tof, stride=bins), :] for b in first]
            given[v, :, at] = jnp.concatenate(held, axis=0).T
            held = [counts[pl.ds(b, tof, stride=bins), :].astype(F32) for b in first]
            counted[v, :, at] = jnp.concatenate(held, axis=0).T
    slices = own * parts
    for v in range(views):
        mix_rows[v * slices:(v + 1) * slices, :] = mix[v].T
    for v in range(views):
        for z in range(own):
            at = (v * own + z) * parts
            mix_t[at:at + parts, :] = mix_rows[pl.ds(v * slices + z, parts, stride=own), :]
    mixes_t = [split(mix_t[v * slices:(v + 1) * slices, :]) for v in range(views)]
    mixes = [split(mix_t[v * slices:(v + 1) * slices, :].T) for v in range(views)]
    for copy in mine_near:
        copy.wait()
    group = lax.broadcasted_iota(jnp.int32, (parts, lanes), 1) // tof

    def swap(held):
        step = own // 2
        while step:
            swapped = list(held)
            low = group // step % 2 == 0
            for g in range(own):
                if g // step % 2 == 0:
                    a, b = held[g], held[g + step]
                    swapped[g] = jnp.where(low, a, pltpu.roll(b, step * tof, 1))
                    swapped[g + step] = jnp.where(low, pltpu.roll(a, lanes - step * tof, 1), b)
            held, step = swapped, step // 2
        return held

    for v in range(views):
        sent(v).wait_recv()
        staged[...] = arrived[v].astype(F32).reshape(staged.shape)
        for n in range(runs):
            at = slice(n * lanes, (n + 1) * lanes)
            held = swap([staged[pl.ds(n * own + g, parts, stride=rank), :] for g in range(own)])
            for z in range(own):
                wide[z * parts:(z + 1) * parts, at] = held[z].astype(BF16)
        total = dot(mixes[v][0], wide[...]) + dot(mixes[v][1], wide[...])
        high, low = split(counted[v] / (given[v] + total))
        spread = dot(mixes_t[v][0], high) + (dot(mixes_t[v][1], high) + dot(mixes_t[v][0], low))
        for n in range(runs):
            at = slice(n * lanes, (n + 1) * lanes)
            held = swap([spread[z * parts:(z + 1) * parts, at] for z in range(own)])
            for g in range(own):
                staged[pl.ds(n * own + g, parts, stride=rank), :] = held[g]
        back[v] = staged[...].reshape(parts, rank, lanes).astype(BF16)
        send_back(v)
    for o in (1, 3, 2):
        for copy in bands(o):
            copy.wait_recv()
        for v in range(views):
            rx_near[o, v] = unpack(rx_in[o - 1, v])
            for b in range(chips):
                ry[o, v, b * width:b * width + reach, b * width:(b + 1) * width] = unpack(ry_in[o - 1, b, v])
    turned = rx_near[...].reshape(chips * views * reach, width).T
    def share(o, v):
        return pltpu.make_async_remote_copy(
            src_ref=back_all.at[0, v], dst_ref=back_all.at[o, v],
            send_sem=share_send.at[o - 1, v], recv_sem=share_recv.at[o - 1, v],
            device_id={"view": peers[o]}, device_id_type=MESH,
        )

    which = lax.broadcasted_iota(jnp.int32, (reach, lanes), 1) // tof

    def project(o, v):
        if o:
            share(o, v).wait_recv()
        held = back_all[o, v].astype(F32).reshape(parts * rank, lanes)
        turn = pltpu.roll(held, lanes // 2, 1)
        pair_of = [held, turn] if v == 0 else [turn, held]
        pair_of = [h.reshape(parts, rank, lanes) for h in pair_of]
        spread_out = jnp.concatenate(pair_of, axis=1).reshape(parts * bins, lanes).astype(BF16)
        weights = tof_near[o].astype(F32)
        chosen = [jnp.where(which == v * own + z, weights, 0.0).astype(BF16) for z in range(own)]
        frames = dot(jnp.concatenate(chosen, axis=0), spread_out, transposed=True).astype(BF16)
        unrotated = dot(frames, ry[o, v, inner, :], transposed=True).astype(BF16)
        at = (o * views + v) * reach
        for z in range(own):
            lines[z, at:at + reach, :] = unrotated[z * reach:(z + 1) * reach]

    for v in range(views):
        sent_back(v).wait_recv()
        for o in (1, 3, 2):
            share(o, v).start()
        project(0, v)
    for v in range(views):
        for o in (1, 3, 2):
            project(o, v)

    def half(at):
        return pl.ds(pl.multiple_of(at * own_rows, own_rows), own_rows)

    def pair(z):
        return pltpu.make_async_remote_copy(
            src_ref=partial.at[z, half(1 - core), :], dst_ref=other.at[z],
            send_sem=pair_send.at[z], recv_sem=pair_recv.at[z], device_id={"view": peers[0]}, device_id_type=MESH,
        )

    for z in range(own):
        partial[z] = dot(turned, lines[z])
        pair(z).start()
    for z in range(own):
        pair(z).wait_recv()
        out_ref[z] = current[z] * (partial[z, half(core), :] + other[z]) / sens[z]
    for v in range(views):
        sent(v).wait_send()
        sent_back(v).wait_send()
    for z in range(own):
        pair(z).wait_send()
    for o in range(1, chips):
        for v in range(views):
            share(o, v).wait_send()
        for copy in bands(o):
            copy.wait_send()


def local(image, sensitivity, resample_x, resample_y, tof_kernel, axial_mix, background, counts):
    parts = lax.axis_size("slab")
    own, own_rows, ny = sensitivity.shape
    views, tof, nx = tof_kernel.shape
    bins, planes = background.shape[2:]
    lanes = own * views * tof
    chips = lax.axis_size("view") // 2
    width = nx // chips
    reach = width + 2 * PAD
    flat = views * tof * bins
    packed = ny // 2
    columns = bins * tof
    vm, dma, i32 = pltpu.VMEM, pltpu.SemaphoreType.DMA, jnp.int32
    hbm = pl.BlockSpec(memory_space=pltpu.HBM)
    return pl.pallas_call(
        kernel,
        out_shape=jax.ShapeDtypeStruct(sensitivity.shape, F32),
        in_specs=[hbm] * 8,
        out_specs=pl.BlockSpec(memory_space=pltpu.VMEM),
        scratch_shapes=[
            vm(image.shape, F32), vm(sensitivity.shape, F32),
            vm((views, nx + 2 * PAD, nx), BF16), vm((chips, views, nx + 2 * PAD, nx), BF16), vm(tof_kernel.shape, BF16),
            vm(axial_mix.shape, F32), vm((flat, planes), F32), vm((flat, planes), i32),
            vm(sensitivity.shape, F32),
            vm((lanes, ny), F32), vm((views, parts, bins // 2, lanes), BF16), vm((views, parts, bins // 2, lanes), BF16),
            vm((views, parts, bins // 2, lanes), BF16), vm((chips, views, parts, bins // 2, lanes), BF16),
            vm((own * parts, columns), BF16),
            vm((views, planes, columns), F32), vm((views, planes, columns), F32),
            vm((packed, lanes), F32),
            vm((views * own * parts, planes), F32), vm((views * own * parts, planes), F32),
            vm((chips, views, reach, width), BF16), vm((nx + 2 * PAD, lanes), BF16), vm((chips, reach, lanes), BF16),
            vm((chips, views, 2 * PIECE, width), BF16), vm((chips, views, 2 * PIECE, width), BF16),
            vm((chips - 1, views, 2 * PIECE, width), BF16), vm((chips - 1, chips, views, 2 * PIECE, width), BF16),
            vm((own, chips * views * reach, ny), BF16), vm((own, width, ny), F32), vm((own, own_rows, ny), F32),
            dma((own + 8,)), dma((views,)), dma((views,)), dma((views,)), dma((views,)),
            dma((own,)), dma((own,)),
            dma((chips - 1, 3)), dma((chips - 1, 3)), dma((chips - 1, views)), dma((chips - 1, views)),
        ],
        compiler_params=pltpu.CompilerParams(collective_id=0, has_side_effects=True, vmem_limit_bytes=48 << 20),
        name="update",
    )(*[
        pltpu.with_memory_space_constraint(a, pltpu.HBM)
        for a in (
            image, sensitivity, resample_x, resample_y, tof_kernel, axial_mix,
            background.reshape(flat, planes), counts.reshape(flat, planes),
        )
    ])


def solution(mesh):
    in_specs = (
        P("slab", None, None),
        P("slab", "view", None),
        P("view", None, None),
        P("view", None, None),
        P("view", None, None),
        P("view", None, None),
        P("view", None, "slab", None),
        P("view", None, "slab", None),
    )
    out_specs = P("slab", "view", None)
    return jax.shard_map(local, mesh=mesh, in_specs=in_specs, out_specs=out_specs, check_vma=False)
```
